32 devices in a mesh: gx: 4 (over y, x), gy: 4 (over z), gz: 2 (over core).
Axes of the slice: x: 2, y: 2, z: 4, core: 2. Of those that a mesh axis runs over, the one named last changes fastest.
Arguments:
- fields: float32 [24, 32, 128, 256], P(None, 'gx', 'gy', 'gz'), may hold values from -8.5 to 8.5
- velocity: float32 [3, 32, 128, 256], P(None, 'gx', 'gy', 'gz'), may hold values from -0.4 to 0.4
- diffusivity: float32 [24], replicated, may hold values from 0.02 to 0.15
- weight_in: bfloat16 [24, 1600], replicated, may hold values from -1.25 to 1.25
- bias_in: float32 [1600], replicated, may hold values from -3 to 3
- weight_mid: bfloat16 [1600, 800], replicated, may hold values from -0.15625 to 0.15625
- bias_mid: float32 [800], replicated, may hold values from -3 to 3
- weight_low: bfloat16 [800, 400], replicated, may hold values from -0.21875 to 0.21875
- bias_low: float32 [400], replicated, may hold values from -3 to 3
- weight_out: bfloat16 [400, 24], replicated, may hold values from -0.3125 to 0.3125
- bias_out: float32 [24], replicated, may hold values from -3 to 3
- react_list: int32 [32, 96], P(('gx', 'gy', 'gz')), may hold values from -1 to 255, as said below
- owner_table: int32 [32, 96], P(('gx', 'gy', 'gz')), may hold values from -1 to 31, as said below
Outputs:
- updated: float32 [24, 32, 128, 256], P(None, 'gx', 'gy', 'gz')
- owner_activity: float32 [32], P(('gx', 'gy', 'gz'))
The draws below stay inside these ranges and needn't reach their ends.
Inputs may be any that keep to these rules, and one draw needn't show every extreme that they name: `react_list`: row d lists distinct blocks of brick d, valid entries first and -1 after them; a brick lists at most 96 blocks and some brick lists exactly 96; all bricks together list 32 times the number of devices. owner_table[d, i] is -1 exactly where react_list[d, i] is, else the owner's index over gx+gy+gz; every device owns exactly 32 blocks; no brick sends more than 3 blocks to one owner, and some brick sends exactly 3 to some owner.
All inputs are finite; a program needn't handle non-finite values.
Results may differ from the reference program's by a relative error of at most 0.00058.
Values may be sent and summed in bfloat16 or wider, within the bound.
A program may use at most 256 MiB of HBM per device.

```python
import math
import jax
import jax.numpy as jnp
from jax import lax

FIELDS = 24
HID_ONE = 1600
HID_TWO = 800
HID_THREE = 400
CX = 8
CY = 32
CZ = 128
OWNED = 32
LIST_MAX = 96
NX = 32
NY = 128
NZ = 256
N_GX = 4
N_GY = 4
N_GZ = 2
DEVICES = 32


def draw_fields(key, part):
    base_key = jax.random.fold_in(key, 11)
    key_scale, key_values = jax.random.split(base_key, 2)
    column_scale = jnp.exp(jax.random.uniform(key_scale, (FIELDS, NX, NY, 1), jnp.float32, jnp.log(0.5), jnp.log(2.0)))
    rough = jnp.clip(jax.random.normal(key_values, (FIELDS, NX, NY, NZ), jnp.float32), -4.0, 4.0)
    return (rough * column_scale).astype(jnp.float32)


def layout(key):
    base_key = jax.random.fold_in(key, 5)
    key_first, key_second, key_place, key_blocks, key_owner = jax.random.split(base_key, 5)
    groups = DEVICES // 4
    spare_blocks = 4 * OWNED - LIST_MAX
    first_share = jax.random.randint(key_first, (groups,), 0, spare_blocks + 1)
    second_share = jax.random.randint(key_second, (groups,), 0, 1 << 20) % (spare_blocks - first_share + 1)
    third_share = spare_blocks - first_share - second_share
    pattern = jnp.stack([jnp.full((groups,), LIST_MAX, jnp.int32), first_share, second_share, third_share], axis=1).reshape(-1).astype(jnp.int32)
    placing = jax.random.permutation(key_place, DEVICES)
    counts = jnp.zeros((DEVICES,), jnp.int32).at[placing].set(pattern)
    block_count = CX * CY
    scores = jax.random.randint(key_blocks, (DEVICES, block_count), 0, 1 << 20) * block_count + jnp.arange(block_count, dtype=jnp.int32)[None, :]
    chosen = jnp.argsort(scores, axis=1)[:, :LIST_MAX].astype(jnp.int32)
    positions = jnp.arange(LIST_MAX, dtype=jnp.int32)[None, :]
    present = positions < counts[:, None]
    starting = jnp.cumsum(counts) - counts
    serial = starting[:, None] + positions
    owners = jax.random.permutation(key_owner, DEVICES).astype(jnp.int32)[serial % DEVICES]
    return (jnp.where(present, chosen, -1).astype(jnp.int32), jnp.where(present, owners, -1).astype(jnp.int32))


def draw_react_list(key, part):
    return layout(key)[0]


def draw_owner_table(key, part):
    return layout(key)[1]


def shard_levels(rng, dims, shards, least, high):
    factor_of = 1.0
    for dim, parts in shards:
        heights = jax.random.uniform(jax.random.fold_in(jax.random.fold_in(rng, 6), dim), (parts,), jnp.float32, least / len(shards), high / len(shards))
        factor_of = factor_of * jnp.repeat(jnp.exp(heights), dims[dim] // parts).reshape((-1,) + (1,) * (len(dims) - 1 - dim))
    return factor_of


def bell_draw(stream_key, extent, deviation, reach, held_as=jnp.bfloat16):
    return jnp.clip(deviation * jax.random.normal(stream_key, extent, jnp.float32), -reach, reach).astype(held_as)


def setup_inputs(seed: int = 0) -> dict:
    key_list = jax.random.split(jax.random.key(seed), 14)
    fields = draw_fields(jax.random.fold_in(key_list[13], 71), 0)
    velocity = jnp.clip(jax.random.uniform(key_list[1], (3, NX, NY, NZ), jnp.float32, -0.4, 0.4) * shard_levels(key_list[1], (3, NX, NY, NZ), ((1, 4), (2, 4), (3, 2)), -0.4, 0.0), -0.4, 0.4)
    diffusivity = jnp.clip(jnp.exp(jax.random.uniform(key_list[2], (FIELDS,), jnp.float32, math.log(0.02), math.log(0.15))), 0.02, 0.15)
    weight_in = bell_draw(key_list[3], (FIELDS, HID_ONE), FIELDS ** -0.5, 1.25)
    bias_in = bell_draw(key_list[4], (HID_ONE,), 0.5, 3.0, jnp.float32)
    weight_mid = bell_draw(key_list[5], (HID_ONE, HID_TWO), HID_ONE ** -0.5, 0.15625)
    bias_mid = bell_draw(key_list[6], (HID_TWO,), 0.5, 3.0, jnp.float32)
    weight_low = bell_draw(key_list[7], (HID_TWO, HID_THREE), HID_TWO ** -0.5, 0.21875)
    bias_low = bell_draw(key_list[8], (HID_THREE,), 0.5, 3.0, jnp.float32)
    weight_out = bell_draw(key_list[9], (HID_THREE, FIELDS), HID_THREE ** -0.5, 0.3125)
    bias_out = bell_draw(key_list[10], (FIELDS,), 0.5, 3.0, jnp.float32)
    react_list = draw_react_list(jax.random.fold_in(key_list[13], 71), 0)
    owner_table = draw_owner_table(jax.random.fold_in(key_list[13], 71), 0)
    return {"fields": fields, "velocity": velocity, "diffusivity": diffusivity, "weight_in": weight_in, "bias_in": bias_in, "weight_mid": weight_mid, "bias_mid": bias_mid, "weight_low": weight_low, "bias_low": bias_low, "weight_out": weight_out, "bias_out": bias_out, "react_list": react_list, "owner_table": owner_table}


viscous = 0.05
third_part = 1.0 / 3.0


def laplace(values_in):
    summed = -6.0 * values_in
    for axis_dim in (1, 2, 3):
        summed = summed + jnp.roll(values_in, -1, axis_dim) + jnp.roll(values_in, 1, axis_dim)
    return summed


def transport(values_in, speeds):
    spread = -6.0 * values_in
    flux_sum = jnp.zeros_like(values_in)
    for axis_dim in (1, 2, 3):
        carried = speeds[axis_dim - 1][None] * values_in
        flux_sum = flux_sum + 0.5 * (jnp.roll(carried, -1, axis_dim) - jnp.roll(carried, 1, axis_dim))
        spread = spread + jnp.roll(values_in, -1, axis_dim) + jnp.roll(values_in, 1, axis_dim)
    return viscous * spread - flux_sum


def network(cell_rows, weight_in, bias_in, weight_mid, bias_mid, weight_low, bias_low, weight_out, bias_out):
    hidden = jax.nn.silu(jnp.dot(cell_rows, weight_in, preferred_element_type=jnp.float32) + bias_in).astype(jnp.bfloat16)
    hidden = jax.nn.silu(jnp.dot(hidden, weight_mid, preferred_element_type=jnp.float32) + bias_mid).astype(jnp.bfloat16)
    hidden = jax.nn.silu(jnp.dot(hidden, weight_low, preferred_element_type=jnp.float32) + bias_low).astype(jnp.bfloat16)
    return jnp.dot(hidden, weight_out, preferred_element_type=jnp.float32) + bias_out


def reference(fields, velocity, diffusivity, weight_in, bias_in, weight_mid, bias_mid, weight_low, bias_low, weight_out, bias_out, react_list, owner_table):
    section_one = fields + transport(fields, velocity)
    section_two = 0.75 * fields + 0.25 * (section_one + transport(section_one, velocity))
    flowed = third_part * fields + (2.0 / 3.0) * (section_two + transport(section_two, velocity))

    devices = N_GX * N_GY * N_GZ
    device = jnp.arange(devices, dtype=jnp.int32)[:, None]
    brick_x = device // (N_GY * N_GZ)
    brick_y = (device // N_GZ) % N_GY
    brick_z = device % N_GZ
    present = react_list >= 0
    clipped = jnp.where(present, react_list, 0).astype(jnp.int32)
    column_x = (brick_x * CX + clipped // CY).reshape(-1).astype(jnp.int32)
    column_y = (brick_y * CY + clipped % CY).reshape(-1).astype(jnp.int32)
    column_z = jnp.broadcast_to(brick_z * CZ, react_list.shape).reshape(-1).astype(jnp.int32)
    ordering = jnp.argsort(jnp.where(present, 0, 1).reshape(-1).astype(jnp.int32), stable=True)[: devices * OWNED]
    column_x = column_x[ordering]
    column_y = column_y[ordering]
    column_z = column_z[ordering]
    owners = owner_table.reshape(-1)[ordering].astype(jnp.int32)

    def fetch_block(start_x, start_y, start_z):
        piece = lax.dynamic_slice(flowed, (jnp.int32(0), start_x, start_y, start_z), (FIELDS, 1, 1, CZ))
        return piece.reshape(FIELDS, CZ)

    blocks = jax.vmap(fetch_block)(column_x, column_y, column_z)
    cell_rows = blocks.astype(jnp.bfloat16).transpose(0, 2, 1).reshape(devices, OWNED * CZ, FIELDS)

    def run_owner(portion):
        return network(portion, weight_in, bias_in, weight_mid, bias_mid, weight_low, bias_low, weight_out, bias_out)

    increments = lax.map(run_owner, cell_rows)
    increments = increments.reshape(devices * OWNED, CZ, FIELDS).transpose(0, 2, 1)
    block_heat = jnp.mean(increments[:, 0, :] ** 2, axis=-1)
    owner_activity = jax.ops.segment_sum(block_heat, owners, num_segments=devices) / 8.0

    offsets = column_z[:, None] + jnp.arange(CZ, dtype=jnp.int32)[None, :]
    reacted = flowed.at[:, column_x[:, None], column_y[:, None], offsets].add(increments.transpose(1, 0, 2))
    updated = reacted + diffusivity[:, None, None, None] * laplace(reacted)
    return updated, owner_activity
```

```python
import functools

import jax
import jax.numpy as jnp
from jax import lax
from jax.experimental import pallas as pl
from jax.experimental.pallas import tpu as pltpu
from jax.sharding import PartitionSpec as P

AXES = ("gx", "gy", "gz")
MESH = pl.DeviceIdType.MESH
SUB = 8
LANES = 128
MIB = 1024 * 1024


def neighbours():
    ids = {a: lax.axis_index(a) for a in AXES}
    out = []
    for a in AXES:
        n = lax.axis_size(a)
        up = dict(ids)
        up[a] = lax.rem(ids[a] + 1, n)
        down = dict(ids)
        down[a] = lax.rem(ids[a] + n - 1, n)
        out.append((tuple(up[b] for b in AXES), tuple(down[b] for b in AXES)))
    return out


def enter(targets):
    barrier = pltpu.get_barrier_semaphore()
    for to in targets:
        pl.semaphore_signal(barrier, inc=1, device_id=to, device_id_type=MESH)
    pl.semaphore_wait(barrier, len(targets))


def peers(axis):
    ids = {a: lax.axis_index(a) for a in AXES}
    n = lax.axis_size(axis)
    out = []
    for k in range(1, n):
        to = dict(ids)
        to[axis] = lax.rem(ids[axis] + k, n)
        out.append(tuple(to[b] for b in AXES))
    return out


def remote(src, dst, send, recv, to):
    return pltpu.make_async_remote_copy(
        src_ref=src, dst_ref=dst, send_sem=send, recv_sem=recv,
        device_id=to, device_id_type=MESH)


def lane_ids():
    return lax.broadcasted_iota(jnp.int32, (SUB, LANES), 1)


class Grid:
    def __init__(self, cx, cy):
        self.cx, self.cy = cx, cy
        self.px, self.py = cx + 2, cy + 2 * SUB
        self.groups = cy // SUB

    def row(self, f, x, y=0):
        return (f * self.px + x + 1) * self.py + SUB + y

    def tile(self, f, x, g):
        r = (f * self.px + x + 1) * self.py + SUB + g * SUB
        return r if isinstance(r, int) else pl.multiple_of(r, SUB)


class Halo:
    def __init__(self, grid, width, near, xs, xr, ys, yr, zs, zr, send_sem, recv_sem):
        self.grid, self.width, self.near = grid, width, near
        self.xs, self.xr, self.ys, self.yr = xs, xr, ys, yr
        self.zs, self.zr, self.send_sem, self.recv_sem = zs, zr, send_sem, recv_sem
        lane = lane_ids()
        self.first, self.last = lane == 0, lane == LANES - 1
        self.even = lax.rem(lane, 2) == 0
        self.pair = lax.rem(lane + 1, LANES) // 2

    def copies(self, slot):
        (xu, xd), (yu, yd), (zu, zd) = self.near
        plan = [
            (self.xs.at[slot, 1], self.xr.at[slot, 0], xu),
            (self.xs.at[slot, 0], self.xr.at[slot, 1], xd),
            (self.ys.at[slot, 1], self.yr.at[slot, 0], yu),
            (self.ys.at[slot, 0], self.yr.at[slot, 1], yd),
            (self.zs.at[slot], self.zr.at[slot, 0], zu),
        ]
        if lax.axis_size("gz") > 2:
            plan.append((self.zs.at[slot], self.zr.at[slot, 1], zd))
        return [
            remote(s, d, self.send_sem.at[slot, i], self.recv_sem.at[slot, i], to)
            for i, (s, d, to) in enumerate(plan)
        ]

    def pack_z(self, face, t, k):
        return jnp.where(self.pair == k, pltpu.roll(t, 2 * k, 1) if k else t, face)

    def z_row(self, slot, x):
        if lax.axis_size("gz") > 2:
            return jnp.where(self.even, self.zr[slot, 1, x], self.zr[slot, 0, x])
        return self.zr[slot, 0, x]

    def z_near(self, t, zrow, k):
        r = pltpu.roll(zrow, LANES - 2 * k, 1) if k else zrow
        after = pltpu.roll(jnp.where(self.first, r, t), LANES - 1, 1)
        before = pltpu.roll(jnp.where(self.last, r, t), 1, 1)
        return after, before

    def send(self, slot, u, base):
        grid = self.grid
        for f in range(self.width):
            for side, x in ((0, 0), (1, grid.cx - 1)):
                self.xs[slot, side, f] = u[
                    pl.ds(grid.tile(base + f, x, 0), grid.cy), :].astype(jnp.bfloat16)
            for side, y in ((0, 0), (1, grid.cy - 1)):
                self.ys[slot, side, f] = u[
                    pl.ds(grid.row(base + f, 0, y), grid.cx, stride=grid.py), :]
        for c in self.copies(slot):
            c.start()

    def load_z(self, slot, u, base):
        grid = self.grid

        def body(x, _):
            face = jnp.zeros((SUB, LANES), jnp.float32)
            for g in range(grid.groups):
                for f in range(self.width):
                    t = u[pl.ds(grid.tile(base + f, x, g), SUB), :]
                    face = self.pack_z(face, t, f * grid.groups + g)
            self.zs[slot, x] = face
            return 0

        lax.fori_loop(0, grid.cx, body, 0)

    def receive(self, slot, u, base):
        grid = self.grid
        for c in self.copies(slot):
            c.wait_recv()
        for f in range(self.width):
            for side, x in ((0, -1), (1, grid.cx)):
                u[pl.ds(grid.tile(base + f, x, 0), grid.cy), :] = self.xr[
                    slot, side, f].astype(jnp.float32)
            for side, y in ((0, -1), (1, grid.cy)):
                u[pl.ds(grid.row(base + f, 0, y), grid.cx, stride=grid.py), :] = self.yr[
                    slot, side, f]

    def finish(self, slot):
        for c in self.copies(slot):
            c.wait_send()


def flow_kernel(nf, cx, cy, q_hbm, v_hbm, out_hbm, u_ref, w_ref, flow_ref, coef,
                vx, vy, vz, vys, vzs, xs, xr, ys, yr, zs, zr,
                send_sem, recv_sem, vs_sem, vr_sem, in_sem, out_sem):
    grid = Grid(cx, cy)
    chunks = nf // SUB
    loads = [pltpu.make_async_copy(
        v_hbm, w_ref.at[:, pl.ds(1, cx), pl.ds(SUB, cy)], in_sem.at[chunks])]
    for c in range(chunks):
        loads.append(pltpu.make_async_copy(
            q_hbm.at[pl.ds(c * SUB, SUB)],
            u_ref.at[0, pl.ds(c * SUB, SUB), pl.ds(1, cx), pl.ds(SUB, cy)], in_sem.at[c]))
    for copy in loads:
        copy.start()
    near = neighbours()
    (xu, xd), (yu, yd), (zu, zd) = near
    halo = Halo(grid, SUB, near, xs, xr, ys, yr, zs, zr, send_sem, recv_sem)
    rows = nf * grid.px * grid.py
    u2 = u_ref.reshape(3 * rows, LANES)
    w2 = w_ref.reshape(3 * grid.px * grid.py, LANES)
    enter([to for pair in near for to in pair])

    loads[0].wait()
    for side, y in ((0, 0), (1, cy - 1)):
        vys[side] = w2[pl.ds(grid.row(1, 0, y), cx, stride=grid.py), :]

    def pack_v(x, _):
        face = jnp.zeros((SUB, LANES), jnp.float32)
        for g in range(grid.groups):
            face = halo.pack_z(face, w2[pl.ds(grid.tile(2, x, g), SUB), :], g)
        vzs[x] = face
        return 0

    lax.fori_loop(0, cx, pack_v, 0)
    plan = [
        (w_ref.at[0, cx, pl.ds(SUB, cy)], vx.at[0], xu),
        (w_ref.at[0, 1, pl.ds(SUB, cy)], vx.at[1], xd),
        (vys.at[1], vy.at[0], yu),
        (vys.at[0], vy.at[1], yd),
        (vzs, vz.at[0], zu),
    ]
    if lax.axis_size("gz") > 2:
        plan.append((vzs, vz.at[1], zd))
    v_copies = [remote(s, d, vs_sem.at[i], vr_sem.at[i], to)
                for i, (s, d, to) in enumerate(plan)]
    for copy in v_copies:
        copy.start()
    for c in range(chunks):
        loads[1 + c].wait()
        halo.load_z(c, u2, c * SUB)
        halo.send(c, u2, c * SUB)

    for copy in v_copies:
        copy.wait_recv()
    for side, x in ((0, -1), (1, cx)):
        w2[pl.ds(grid.tile(0, x, 0), cy), :] = vx[side]
    for side, y in ((0, -1), (1, cy)):
        w2[pl.ds(grid.row(1, 0, y), cx, stride=grid.py), :] = vy[side]

    def make_coef(x, _):
        if lax.axis_size("gz") > 2:
            zrow = jnp.where(halo.even, vz[1, x], vz[0, x])
        else:
            zrow = vz[0, x]
        for g in range(grid.groups):
            r0 = grid.tile(0, x, g)
            r1 = grid.tile(1, x, g)
            after, before = halo.z_near(w2[pl.ds(grid.tile(2, x, g), SUB), :], zrow, g)
            values = (
                0.05 - 0.5 * w2[pl.ds(r0 + grid.py, SUB), :],
                0.05 + 0.5 * w2[pl.ds(r0 - grid.py, SUB), :],
                0.05 - 0.5 * w2[pl.ds(r1 + 1, SUB), :],
                0.05 + 0.5 * w2[pl.ds(r1 - 1, SUB), :],
                0.05 - 0.5 * after,
                0.05 + 0.5 * before,
            )
            for i, value in enumerate(values):
                coef[i, x, g] = value
        return 0

    lax.fori_loop(0, cx, make_coef, 0)

    def stencil(zrow, ks, row, k):
        t = u2[pl.ds(row, SUB), :]
        za, zb = halo.z_near(t, zrow, k)
        s = ks[0] * u2[pl.ds(row + grid.py, SUB), :] + ks[1] * u2[pl.ds(row - grid.py, SUB), :]
        s = s + (ks[2] * u2[pl.ds(row + 1, SUB), :] + ks[3] * u2[pl.ds(row - 1, SUB), :])
        return t, s + (ks[4] * za + ks[5] * zb)

    stores = []
    for stage in range(3):
        weight = (1.0 / 3.0, 0.5, 1.0)[stage]
        for c in range(chunks):
            slot = stage * chunks + c
            first = stage * nf + c * SUB
            halo.receive(slot, u2, first)

            def body(x, _):
                zrow = halo.z_row(slot, x)
                face = jnp.zeros((SUB, LANES), jnp.float32)
                for g in range(grid.groups):
                    ks = [coef[i, x, g] for i in range(6)]
                    for f in range(SUB):
                        k = f * grid.groups + g
                        t, s = stencil(zrow, ks, grid.tile(first + f, x, g), k)
                        q = u2[pl.ds(grid.tile(c * SUB + f, x, g), SUB), :]
                        r = q + weight * (s - 0.3 * t)
                        if stage == 2:
                            flow_ref[c * SUB + f, x, pl.ds(g * SUB, SUB)] = r
                        else:
                            u2[pl.ds(grid.tile(first + nf + f, x, g), SUB), :] = r
                            face = halo.pack_z(face, r, k)
                if stage < 2:
                    zs[slot + chunks, x] = face
                return 0

            lax.fori_loop(0, cx, body, 0)
            if stage < 2:
                halo.send(slot + chunks, u2, first + nf)
            else:
                part = pl.ds(c * SUB, SUB)
                stores.append(pltpu.make_async_copy(
                    flow_ref.at[part], out_hbm.at[part], out_sem.at[c]))
                stores[-1].start()
    for copy in v_copies:
        copy.wait_send()
    for slot in range(3 * chunks):
        halo.finish(slot)
    for copy in stores:
        copy.wait()


def diffuse_kernel(nf, cx, cy, d_ref, q_hbm, act_in, out_hbm, act_out, u_ref, new_ref, part,
                   got, act_send, act_recv, xs, xr, ys, yr, zs, zr, send_sem, recv_sem,
                   in_sem, out_sem):
    grid = Grid(cx, cy)
    chunks = nf // SUB
    loads = []
    for c in range(chunks):
        loads.append(pltpu.make_async_copy(
            q_hbm.at[pl.ds(c * SUB, SUB)],
            u_ref.at[pl.ds(c * SUB, SUB), pl.ds(1, cx), pl.ds(SUB, cy)], in_sem.at[c]))
        loads[-1].start()
    near = neighbours()
    groups = [peers(a) for a in AXES[::-1]]
    enter([to for g in groups for to in g])
    halo = Halo(grid, SUB, near, xs, xr, ys, yr, zs, zr, send_sem, recv_sem)
    lane = lane_ids()
    u2 = u_ref.reshape(nf * grid.px * grid.py, LANES)

    def hops(phase):
        return [remote(part.at[phase], got.at[phase, k], act_send.at[phase, k],
                       act_recv.at[phase, k], to)
                for k, to in enumerate(groups[phase])]

    def gather(phase):
        for h in hops(phase):
            h.wait_recv()
        total = part[phase]
        for k in range(len(groups[phase])):
            total = total + got[phase, k]
        return total

    part[0] = act_in[...]
    for c in range(chunks):
        loads[c].wait()
        halo.load_z(c, u2, c * SUB)
        halo.send(c, u2, c * SUB)
        if c == 0:
            for h in hops(0):
                h.start()
    stores = []
    for c in range(chunks):
        if c < len(groups) - 1:
            part[c + 1] = gather(c)
            for h in hops(c + 1):
                h.start()
        first = c * SUB
        halo.receive(c, u2, first)

        def body(x, _):
            zrow = halo.z_row(c, x)
            for f in range(SUB):
                rate = d_ref[first + f]
                for g in range(grid.groups):
                    row = grid.tile(first + f, x, g)
                    t = u2[pl.ds(row, SUB), :]
                    za, zb = halo.z_near(t, zrow, f * grid.groups + g)
                    s = u2[pl.ds(row + grid.py, SUB), :] + u2[pl.ds(row - grid.py, SUB), :]
                    s = s + (u2[pl.ds(row + 1, SUB), :] + u2[pl.ds(row - 1, SUB), :])
                    s = s + (za + zb)
                    new_ref[first + f, x, pl.ds(g * SUB, SUB)] = t + rate * (s - 6.0 * t)
            return 0

        lax.fori_loop(0, cx, body, 0)
        chunk = pl.ds(first, SUB)
        stores.append(pltpu.make_async_copy(new_ref.at[chunk], out_hbm.at[chunk], out_sem.at[c]))
        stores[-1].start()
    done = min(chunks, len(groups) - 1)
    for phase in range(done, len(groups) - 1):
        part[phase + 1] = gather(phase)
        for h in hops(phase + 1):
            h.start()
    total = gather(len(groups) - 1)
    me = (lax.axis_index("gx") * lax.axis_size("gy") + lax.axis_index("gy")) * lax.axis_size(
        "gz") + lax.axis_index("gz")
    flat = lax.broadcasted_iota(jnp.int32, (SUB, LANES), 0) * LANES + lane
    act_out[0] = jnp.sum(jnp.where(flat == me, total, 0.0))
    for phase in range(len(groups)):
        for h in hops(phase):
            h.wait_send()
    for c in range(chunks):
        halo.finish(c)
    for copy in stores:
        copy.wait()


def widen(dst, weight, scale, cols):
    k = weight.shape[1]
    dst[:, :k] = weight[...] * jnp.bfloat16(scale)
    dst[:, k:] = cols


def chem_kernel(nf, cells, group, list_ref, owner_ref, q_ref, w1, w2_in, w3_in, w4_in, cols,
                out_ref, act_ref, w2, w3, w4, x_in, h1, h2, h3, inc):
    listed = list_ref.shape[0]
    n_lanes = group * LANES
    chunks = nf // SUB
    out_ref[...] = q_ref[...]
    act_ref[...] = jnp.zeros_like(act_ref)
    n2, n3, n4 = w2.shape[0], w3.shape[0], w4.shape[0]
    widen(w2, w2_in, 0.5, cols[:n2])
    widen(w3, w3_in, 0.5, cols[n2:n2 + n3])
    widen(w4, w4_in, 1.0, cols[n2 + n3:])
    flat = (lax.broadcasted_iota(jnp.int32, (SUB, LANES), 0) * LANES + lane_ids())
    row = lax.broadcasted_iota(jnp.int32, (16, n_lanes), 0)
    ones = jnp.where(row < 3, 1.0, 0.0)
    x_in[nf:nf + SUB] = ones[:SUB]
    for h in (h1, h2, h3):
        h[h.shape[0] - 16:] = ones.astype(jnp.bfloat16)
    count = lax.fori_loop(
        0, listed, lambda i, n: n + jnp.where(list_ref[i] >= 0, 1, 0), 0)

    def layer(w, src, dst, step):
        rows = w.shape[0]
        for m in range(0, rows, step):
            k = min(step, rows - m)
            h = jnp.dot(w[m:m + k], src, preferred_element_type=jnp.float32)
            dst[m:m + k] = (h + h * jnp.tanh(h)).astype(jnp.bfloat16)

    def run(g, _):
        base = g * group
        for i in range(group):
            b = jnp.maximum(list_ref[base + i], 0)
            for c in range(chunks):
                x_in[c * SUB:(c + 1) * SUB, i * LANES:(i + 1) * LANES] = q_ref[
                    pl.ds(c * SUB * cells + b, SUB, stride=cells), :]
        layer(w1, x_in[...].astype(jnp.bfloat16), h1, 400)
        layer(w2, h1[...], h2, 400)
        layer(w3, h2[...], h3, 400)
        inc[...] = jnp.dot(w4[...], h3[...], preferred_element_type=jnp.float32)
        for i in range(group):
            entry = list_ref[base + i]
            b = jnp.maximum(entry, 0)
            valid = jnp.where(entry >= 0, 1.0, 0.0)
            for c in range(chunks):
                t = inc[c * SUB:(c + 1) * SUB, i * LANES:(i + 1) * LANES]
                where = pl.ds(c * SUB * cells + b, SUB, stride=cells)
                out_ref[where, :] = out_ref[where, :] + valid * t
            r = inc[0:1, i * LANES:(i + 1) * LANES]
            heat = jnp.sum(r * r, axis=1, keepdims=True) * (valid / (8.0 * LANES))
            act_ref[...] = act_ref[...] + jnp.where(flat == owner_ref[base + i], heat, 0.0)
        return 0

    lax.fori_loop(0, (count + group - 1) // group, run, 0)


def bias_columns(bias, width):
    rest = bias
    parts = []
    for _ in range(3):
        part = lax.reduce_precision(rest, 8, 7)
        rest = rest - part
        parts.append(part)
    lane = lax.broadcasted_iota(jnp.int32, (bias.shape[0], width), 1)
    out = jnp.zeros((bias.shape[0], width), jnp.float32)
    for i, part in enumerate(parts):
        out = jnp.where(lane == i, part[:, None], out)
    return out.astype(jnp.bfloat16)


def halo_scratch(slots, cx, cy):
    return [
        pltpu.VMEM((slots, 2, SUB, cy, LANES), jnp.bfloat16),
        pltpu.VMEM((slots, 2, SUB, cy, LANES), jnp.bfloat16),
        pltpu.VMEM((slots, 2, SUB, cx, LANES), jnp.float32),
        pltpu.VMEM((slots, 2, SUB, cx, LANES), jnp.float32),
        pltpu.VMEM((slots, cx, SUB, LANES), jnp.float32),
        pltpu.VMEM((slots, 2, cx, SUB, LANES), jnp.float32),
        pltpu.SemaphoreType.DMA((slots, 6)),
        pltpu.SemaphoreType.DMA((slots, 6)),
    ]


def spec(space, n=1):
    return [pl.BlockSpec(memory_space=space)] * n


def local(fields, velocity, diffusivity, weight_in, bias_in, weight_mid, bias_mid,
          weight_low, bias_low, weight_out, bias_out, react_list, owner_table):
    nf, cx, cy, cz = fields.shape
    chunks = nf // SUB
    cells = cx * cy
    padded = (cx + 2, cy + 2 * SUB, cz)
    slots = 3 * chunks
    dma = pltpu.SemaphoreType.DMA
    halos = halo_scratch(slots, cx, cy)
    flowed = pl.pallas_call(
        functools.partial(flow_kernel, nf, cx, cy),
        out_shape=jax.ShapeDtypeStruct(fields.shape, jnp.float32),
        in_specs=spec(pl.ANY, 2),
        out_specs=spec(pl.ANY)[0],
        scratch_shapes=[
            pltpu.VMEM((3, nf) + padded, jnp.float32),
            pltpu.VMEM((3,) + padded, jnp.float32),
            pltpu.VMEM((nf, cx, cy, cz), jnp.float32),
            pltpu.VMEM((6, cx, cy // SUB, SUB, cz), jnp.float32),
            pltpu.VMEM((2, cy, cz), jnp.float32),
            pltpu.VMEM((2, cx, cz), jnp.float32),
            pltpu.VMEM((2, cx, SUB, cz), jnp.float32),
            pltpu.VMEM((2, cx, cz), jnp.float32),
            pltpu.VMEM((cx, SUB, cz), jnp.float32),
        ] + halos + [dma((6,)), dma((6,)), dma((chunks + 1,)), dma((chunks,))],
        compiler_params=pltpu.CompilerParams(
            collective_id=0, has_side_effects=True, vmem_limit_bytes=40 * MIB),
        name="flow",
    )(fields, velocity)

    group = 4
    h = (weight_in.shape[1], weight_mid.shape[1], weight_low.shape[1])
    half = jnp.bfloat16(0.5)
    w1 = jnp.concatenate([weight_in.T * half, bias_columns(bias_in * 0.5, SUB)], axis=1)
    cols = bias_columns(
        jnp.concatenate([bias_mid * 0.5, bias_low * 0.5, bias_out]), 16)
    n_lanes = group * LANES
    reacted, activity = pl.pallas_call(
        functools.partial(chem_kernel, nf, cells, group),
        out_shape=(jax.ShapeDtypeStruct((nf * cells, cz), jnp.float32),
                   jax.ShapeDtypeStruct((SUB, LANES), jnp.float32)),
        in_specs=spec(pltpu.SMEM, 2) + spec(pltpu.VMEM, 6),
        out_specs=tuple(spec(pltpu.VMEM, 2)),
        scratch_shapes=[
            pltpu.VMEM((h[1], h[0] + 16), jnp.bfloat16),
            pltpu.VMEM((h[2], h[1] + 16), jnp.bfloat16),
            pltpu.VMEM((nf, h[2] + 16), jnp.bfloat16),
            pltpu.VMEM((nf + SUB, n_lanes), jnp.float32),
            pltpu.VMEM((h[0] + 16, n_lanes), jnp.bfloat16),
            pltpu.VMEM((h[1] + 16, n_lanes), jnp.bfloat16),
            pltpu.VMEM((h[2] + 16, n_lanes), jnp.bfloat16),
            pltpu.VMEM((nf, n_lanes), jnp.float32),
        ],
        compiler_params=pltpu.CompilerParams(vmem_limit_bytes=40 * MIB),
        name="chem",
    )(react_list[0], owner_table[0], flowed.reshape(nf * cells, cz), w1,
      weight_mid.T, weight_low.T, weight_out.T, cols)

    most = max(lax.axis_size(a) for a in AXES) - 1
    updated, mine = pl.pallas_call(
        functools.partial(diffuse_kernel, nf, cx, cy),
        out_shape=(jax.ShapeDtypeStruct(fields.shape, jnp.float32),
                   jax.ShapeDtypeStruct((1,), jnp.float32)),
        in_specs=spec(pltpu.SMEM) + spec(pl.ANY) + spec(pltpu.VMEM),
        out_specs=(spec(pl.ANY)[0], spec(pltpu.SMEM)[0]),
        scratch_shapes=[
            pltpu.VMEM((nf,) + padded, jnp.float32),
            pltpu.VMEM((nf, cx, cy, cz), jnp.float32),
            pltpu.VMEM((len(AXES), SUB, LANES), jnp.float32),
            pltpu.VMEM((len(AXES), most, SUB, LANES), jnp.float32),
            dma((len(AXES), most)),
            dma((len(AXES), most)),
        ] + halo_scratch(chunks, cx, cy) + [dma((chunks,)), dma((chunks,))],
        compiler_params=pltpu.CompilerParams(
            collective_id=1, has_side_effects=True, vmem_limit_bytes=40 * MIB),
        name="diffuse",
    )(diffusivity, reacted.reshape(fields.shape), activity)
    return updated, mine


def solution(mesh):
    return jax.shard_map(
        local,
        mesh=mesh,
        in_specs=(P(None, *AXES), P(None, *AXES)) + (P(),) * 9
        + (P(AXES, None), P(AXES, None)),
        out_specs=(P(None, *AXES), P(AXES)),
        check_vma=False,
    )
```

```python
import functools

import jax
import jax.numpy as jnp
from jax import lax
from jax.experimental import pallas as pl
from jax.experimental.pallas import tpu as pltpu
from jax.sharding import PartitionSpec as P

AXES = ("gx", "gy", "gz")
MESH = pl.DeviceIdType.MESH
SUB = 8
LANES = 128
MIB = 1024 * 1024


def neighbours():
    ids = {a: lax.axis_index(a) for a in AXES}
    out = []
    for a in AXES:
        n = lax.axis_size(a)
        up = dict(ids)
        up[a] = lax.rem(ids[a] + 1, n)
        down = dict(ids)
        down[a] = lax.rem(ids[a] + n - 1, n)
        out.append((tuple(up[b] for b in AXES), tuple(down[b] for b in AXES)))
    return out


def enter(targets):
    barrier = pltpu.get_barrier_semaphore()
    for to in targets:
        pl.semaphore_signal(barrier, inc=1, device_id=to, device_id_type=MESH)
    pl.semaphore_wait(barrier, len(targets))


def peers(axis):
    ids = {a: lax.axis_index(a) for a in AXES}
    n = lax.axis_size(axis)
    out = []
    for k in range(1, n):
        to = dict(ids)
        to[axis] = lax.rem(ids[axis] + k, n)
        out.append(tuple(to[b] for b in AXES))
    return out


def remote(src, dst, send, recv, to):
    return pltpu.make_async_remote_copy(
        src_ref=src, dst_ref=dst, send_sem=send, recv_sem=recv,
        device_id=to, device_id_type=MESH)


def lane_ids():
    return lax.broadcasted_iota(jnp.int32, (SUB, LANES), 1)


class Grid:
    def __init__(self, cx, cy):
        self.cx, self.cy = cx, cy
        self.px, self.py = cx + 2, cy + 2 * SUB
        self.groups = cy // SUB

    def row(self, f, x, y=0):
        return (f * self.px + x + 1) * self.py + SUB + y

    def tile(self, f, x, g):
        r = (f * self.px + x + 1) * self.py + SUB + g * SUB
        return r if isinstance(r, int) else pl.multiple_of(r, SUB)


class Halo:
    def __init__(self, grid, width, near, xs, xr, ys, yr, zs, zr, send_sem, recv_sem):
        self.grid, self.width, self.near = grid, width, near
        self.xs, self.xr, self.ys, self.yr = xs, xr, ys, yr
        self.zs, self.zr, self.send_sem, self.recv_sem = zs, zr, send_sem, recv_sem
        lane = lane_ids()
        self.first, self.last = lane == 0, lane == LANES - 1
        self.even = lax.rem(lane, 2) == 0
        self.pair = lax.rem(lane + 1, LANES) // 2

    def copies(self, slot):
        (xu, xd), (yu, yd), (zu, zd) = self.near
        plan = [
            (self.xs.at[slot, 1], self.xr.at[slot, 0], xu),
            (self.xs.at[slot, 0], self.xr.at[slot, 1], xd),
            (self.ys.at[slot, 1], self.yr.at[slot, 0], yu),
            (self.ys.at[slot, 0], self.yr.at[slot, 1], yd),
            (self.zs.at[slot], self.zr.at[slot, 0], zu),
        ]
        if lax.axis_size("gz") > 2:
            plan.append((self.zs.at[slot], self.zr.at[slot, 1], zd))
        return [
            remote(s, d, self.send_sem.at[slot, i], self.recv_sem.at[slot, i], to)
            for i, (s, d, to) in enumerate(plan)
        ]

    def pack_z(self, face, t, k):
        return jnp.where(self.pair == k, pltpu.roll(t, 2 * k, 1) if k else t, face)

    def z_row(self, slot, x):
        if lax.axis_size("gz") > 2:
            return jnp.where(self.even, self.zr[slot, 1, x], self.zr[slot, 0, x])
        return self.zr[slot, 0, x]

    def z_near(self, t, zrow, k):
        r = pltpu.roll(zrow, LANES - 2 * k, 1) if k else zrow
        after = pltpu.roll(jnp.where(self.first, r, t), LANES - 1, 1)
        before = pltpu.roll(jnp.where(self.last, r, t), 1, 1)
        return after, before

    def send(self, slot, u, base):
        grid = self.grid
        for f in range(self.width):
            for side, x in ((0, 0), (1, grid.cx - 1)):
                self.xs[slot, side, f] = u[
                    pl.ds(grid.tile(base + f, x, 0), grid.cy), :].astype(jnp.bfloat16)
            for side, y in ((0, 0), (1, grid.cy - 1)):
                self.ys[slot, side, f] = u[
                    pl.ds(grid.row(base + f, 0, y), grid.cx, stride=grid.py), :]
        for c in self.copies(slot):
            c.start()

    def load_z(self, slot, u, base):
        grid = self.grid

        def body(x, _):
            face = jnp.zeros((SUB, LANES), jnp.float32)
            for g in range(grid.groups):
                for f in range(self.width):
                    t = u[pl.ds(grid.tile(base + f, x, g), SUB), :]
                    face = self.pack_z(face, t, f * grid.groups + g)
            self.zs[slot, x] = face
            return 0

        lax.fori_loop(0, grid.cx, body, 0)

    def receive(self, slot, u, base):
        grid = self.grid
        for c in self.copies(slot):
            c.wait_recv()
        for f in range(self.width):
            for side, x in ((0, -1), (1, grid.cx)):
                u[pl.ds(grid.tile(base + f, x, 0), grid.cy), :] = self.xr[
                    slot, side, f].astype(jnp.float32)
            for side, y in ((0, -1), (1, grid.cy)):
                u[pl.ds(grid.row(base + f, 0, y), grid.cx, stride=grid.py), :] = self.yr[
                    slot, side, f]

    def finish(self, slot):
        for c in self.copies(slot):
            c.wait_send()


class Team:
    def __init__(self):
        self.nx, self.ny, self.nz = (lax.axis_size(a) for a in AXES)
        self.span = 2 if self.ny % 2 == 0 else self.ny
        self.size = self.nx * self.span * self.nz

    def slots(self, listed):
        return 2 * ((listed + 2 * self.size - 1) // (2 * self.size))

    def place(self):
        i, j, k = (lax.axis_index(a) for a in AXES)
        return (i * self.span + lax.rem(j, self.span)) * self.nz + k

    def member(self, step):
        m = lax.rem(self.place() + step, self.size)
        i = m // (self.span * self.nz)
        j = lax.rem(m // self.nz, self.span)
        j = j + (lax.axis_index("gy") // self.span) * self.span
        return (i, j, lax.rem(m, self.nz))


def bias_rows(dst, row, lane, bias, scale):
    n = bias.shape[0]
    rest = bias[...].reshape(1, n) * scale
    for i in range(3):
        part = rest.astype(jnp.bfloat16).astype(jnp.float32)
        rest = rest - part
        dst[row + i:row + i + 1, lane:lane + n] = part


def turned(dst, src):
    for j in range(0, src.shape[1], LANES):
        dst[j:j + LANES] = src[:, j:j + LANES].T.astype(jnp.bfloat16)


def widen(dst, src, scale, cols, first):
    rows, k = src.shape
    step = 16 if rows % 16 == 0 else rows

    def body(j, _):
        at = pl.ds(pl.multiple_of(j * step, step), step)
        dst[at, pl.ds(0, k)] = src[at, :] * jnp.bfloat16(scale)
        dst[at, pl.ds(k, 16)] = cols[pl.ds(pl.multiple_of(first + j * step, 8), step),
                                     pl.ds(0, 16)]
        return 0

    lax.fori_loop(0, rows // step, body, 0)


def up(n, m):
    return (n + m - 1) // m * m


def flow_kernel(nf, cx, cy, list_hbm, q_hbm, v_hbm, wi_hbm, wm_hbm, wl_hbm, wo_hbm,
                b1_hbm, b2_hbm, b3_hbm, b4_hbm,
                out_hbm, slot_hbm, count_hbm, rest_hbm, w1_hbm, w2_hbm, w3_hbm, w4_hbm,
                list_ref, u0, u1, u2, w_ref, flow_ref, coef, sd, rv, cs, cr,
                wi, wm, wl, wo, b1, b2, b3, b4, t1, t2, cols, w1, w2, w3, w4,
                h1, h2, h3, rest,
                vx, vy, vz, vys, vzs, xs, xr, ys, yr, zs, zr,
                send_sem, recv_sem, vs_sem, vr_sem, in_sem, out_sem,
                team_send, team_recv, w_in, w_out, back_sem):
    grid = Grid(cx, cy)
    chunks = nf // SUB
    cells = cx * cy
    team = Team()
    listed = list_ref.shape[1]
    loads = [pltpu.make_async_copy(
        v_hbm, w_ref.at[:, pl.ds(1, cx), pl.ds(SUB, cy)], in_sem.at[chunks])]
    for c in range(chunks):
        loads.append(pltpu.make_async_copy(
            q_hbm.at[pl.ds(c * SUB, SUB)],
            u0.at[pl.ds(c * SUB, SUB), pl.ds(1, cx), pl.ds(SUB, cy)], in_sem.at[c]))
    for i, (src, dst) in enumerate((
            (wi_hbm, wi), (b1_hbm, b1), (b2_hbm, b2), (b3_hbm, b3), (b4_hbm, b4),
            (wo_hbm, wo), (list_hbm, list_ref), (wl_hbm, wl), (wm_hbm, wm))):
        loads.append(pltpu.make_async_copy(src, dst, w_in.at[i]))
    for copy in loads:
        copy.start()
    w_loads = loads[1 + chunks:]
    near = neighbours()
    (xu, xd), (yu, yd), (zu, zd) = near
    halo = Halo(grid, SUB, near, xs, xr, ys, yr, zs, zr, send_sem, recv_sem)
    rows = nf * grid.px * grid.py
    us = [u.reshape(rows, LANES) for u in (u0, u1, u2)]
    vv = w_ref.reshape(3 * grid.px * grid.py, LANES)
    members = [team.member(k) for k in range(team.size)]
    enter([to for pair in near for to in pair] + members[1:])

    loads[0].wait()
    for side, y in ((0, 0), (1, cy - 1)):
        vys[side] = vv[pl.ds(grid.row(1, 0, y), cx, stride=grid.py), :]

    def pack_v(x, _):
        face = jnp.zeros((SUB, LANES), jnp.float32)
        for g in range(grid.groups):
            face = halo.pack_z(face, vv[pl.ds(grid.tile(2, x, g), SUB), :], g)
        vzs[x] = face
        return 0

    lax.fori_loop(0, cx, pack_v, 0)
    plan = [
        (w_ref.at[0, cx, pl.ds(SUB, cy)], vx.at[0], xu),
        (w_ref.at[0, 1, pl.ds(SUB, cy)], vx.at[1], xd),
        (vys.at[1], vy.at[0], yu),
        (vys.at[0], vy.at[1], yd),
        (vzs, vz.at[0], zu),
    ]
    if lax.axis_size("gz") > 2:
        plan.append((vzs, vz.at[1], zd))
    v_copies = [remote(s, d, vs_sem.at[i], vr_sem.at[i], to)
                for i, (s, d, to) in enumerate(plan)]
    for copy in v_copies:
        copy.start()
    for c in range(chunks):
        loads[1 + c].wait()
        halo.load_z(c, us[0], c * SUB)
        halo.send(c, us[0], c * SUB)

    for copy in w_loads:
        copy.wait()
    count = lax.fori_loop(
        0, listed, lambda i, n: n + jnp.where(list_ref[0, i] >= 0, 1, 0), 0)
    cs[...] = jnp.full((1, LANES), count, jnp.int32)
    cr[0] = cs[...]
    counts = [remote(cs, cr.at[k], team_send.at[chunks, k], team_recv.at[chunks, k], members[k])
              for k in range(1, team.size)]
    for copy in counts:
        copy.start()

    t1[...] = jnp.zeros_like(t1)
    t2[...] = jnp.zeros_like(t2)
    n2, n3 = up(w2.shape[0], LANES), up(w3.shape[0], LANES)
    t1[0:nf, 0:wi.shape[1]] = wi[...].astype(jnp.float32) * 0.5
    bias_rows(t1, nf, 0, b1, 0.5)
    bias_rows(t2, 0, 0, b2, 0.5)
    bias_rows(t2, 0, n2, b3, 0.5)
    bias_rows(t2, 0, n2 + n3, b4, 1.0)
    turned(w1, t1)
    turned(cols, t2)
    widen(w2, wm, 0.5, cols, 0)
    widen(w3, wl, 0.5, cols, n2)
    widen(w4, wo, 1.0, cols, n2 + n3)
    for h in (h1, h2, h3):
        h[h.shape[0] - 16:] = bias_ones(16, LANES).astype(jnp.bfloat16)
    origin = jnp.concatenate(
        [jnp.zeros((nf, LANES), jnp.float32), bias_ones(w1.shape[1] - nf, LANES)], axis=0)
    rest[...] = network(origin.astype(jnp.bfloat16), w1, w2, w3, w4, h1, h2, h3)
    stores = [pltpu.make_async_copy(src, dst, w_out.at[i]) for i, (src, dst) in enumerate(
        ((rest, rest_hbm), (w1, w1_hbm), (w2, w2_hbm), (w3, w3_hbm), (w4, w4_hbm)))]
    for copy in stores:
        copy.start()

    for copy in v_copies:
        copy.wait_recv()
    for side, x in ((0, -1), (1, cx)):
        vv[pl.ds(grid.tile(0, x, 0), cy), :] = vx[side]
    for side, y in ((0, -1), (1, cy)):
        vv[pl.ds(grid.row(1, 0, y), cx, stride=grid.py), :] = vy[side]

    def make_coef(x, _):
        if lax.axis_size("gz") > 2:
            zrow = jnp.where(halo.even, vz[1, x], vz[0, x])
        else:
            zrow = vz[0, x]
        for g in range(grid.groups):
            r0 = grid.tile(0, x, g)
            r1 = grid.tile(1, x, g)
            after, before = halo.z_near(vv[pl.ds(grid.tile(2, x, g), SUB), :], zrow, g)
            values = (
                0.05 - 0.5 * vv[pl.ds(r0 + grid.py, SUB), :],
                0.05 + 0.5 * vv[pl.ds(r0 - grid.py, SUB), :],
                0.05 - 0.5 * vv[pl.ds(r1 + 1, SUB), :],
                0.05 + 0.5 * vv[pl.ds(r1 - 1, SUB), :],
                0.05 - 0.5 * after,
                0.05 + 0.5 * before,
            )
            for i, value in enumerate(values):
                coef[i, x, g] = value
        return 0

    lax.fori_loop(0, cx, make_coef, 0)

    flow2 = flow_ref.reshape(nf * cells, LANES)
    sends = []

    def block(c, e):
        b = jnp.maximum(list_ref[0, min(e, listed - 1)], 0)
        return flow2[pl.ds(c * SUB * cells + b, SUB, stride=cells), :]

    def dispatch(c):
        for k in range(team.size):
            dst = sd if k else rv
            for p in range(sd.shape[2]):
                pair = [block(c, (2 * p + h) * team.size + k) for h in range(2)]
                dst[c, k, p] = jnp.concatenate(pair, axis=0).astype(jnp.bfloat16)
        for k in range(1, team.size):
            sends.append(remote(sd.at[c, k], rv.at[c, k], team_send.at[c, k],
                                team_recv.at[c, k], members[k]))
            sends[-1].start()

    for stage in range(3):
        weight = (1.0 / 3.0, 0.5, 1.0)[stage]
        u = us[stage]
        for c in range(chunks):
            slot = stage * chunks + c
            first = c * SUB
            halo.receive(slot, u, first)

            def body(x, _):
                zrow = halo.z_row(slot, x)
                face = jnp.zeros((SUB, LANES), jnp.float32)
                for g in range(grid.groups):
                    ks = [coef[i, x, g] for i in range(6)]
                    for f in range(SUB):
                        k = f * grid.groups + g
                        row = grid.tile(first + f, x, g)
                        t = u[pl.ds(row, SUB), :]
                        za, zb = halo.z_near(t, zrow, k)
                        s = (ks[0] * u[pl.ds(row + grid.py, SUB), :]
                             + ks[1] * u[pl.ds(row - grid.py, SUB), :])
                        s = s + (ks[2] * u[pl.ds(row + 1, SUB), :]
                                 + ks[3] * u[pl.ds(row - 1, SUB), :])
                        s = s + (ks[4] * za + ks[5] * zb)
                        q = t if stage == 0 else us[0][pl.ds(row, SUB), :]
                        r = q + weight * (s - 0.3 * t)
                        if stage == 2:
                            flow_ref[first + f, x, pl.ds(g * SUB, SUB)] = r
                        else:
                            us[stage + 1][pl.ds(row, SUB), :] = r
                            face = halo.pack_z(face, r, k)
                if stage < 2:
                    zs[slot + chunks, x] = face
                return 0

            lax.fori_loop(0, cx, body, 0)
            if stage < 2:
                halo.send(slot + chunks, us[stage + 1], first)
            else:
                dispatch(c)
                part = pl.ds(first, SUB)
                stores.append(pltpu.make_async_copy(
                    flow_ref.at[part], out_hbm.at[part], out_sem.at[c]))
                stores[-1].start()
    for copy in counts + sends:
        copy.wait_recv()
    backs = [pltpu.make_async_copy(cr, count_hbm, back_sem.at[0]),
             pltpu.make_async_copy(rv, slot_hbm, back_sem.at[1])]
    for copy in backs:
        copy.start()
    for copy in v_copies + counts + sends:
        copy.wait_send()
    for slot in range(3 * chunks):
        halo.finish(slot)
    for copy in stores + backs:
        copy.wait()


def layer(w, src, dst, step):
    rows = dst.shape[0] - 16
    for m in range(0, rows, step):
        k = min(step, rows - m)
        h = jnp.dot(w[m:m + k], src, preferred_element_type=jnp.float32)
        dst[m:m + k] = (h + h * jnp.tanh(h)).astype(jnp.bfloat16)


def network(x, w1, w2, w3, w4, h1, h2, h3):
    layer(w1, x, h1, 400)
    layer(w2, h1[...], h2, 400)
    layer(w3, h2[...], h3, 400)
    return jnp.dot(w4[...], h3[...], preferred_element_type=jnp.float32)


def bias_ones(rows, lanes):
    return jnp.where(lax.broadcasted_iota(jnp.int32, (rows, lanes), 0) < 3, 1.0, 0.0)


def chem_kernel(nf, cells, group, size, list_ref, count_ref, slots, rest, w1, w2, w3,
                w4, ret_ref, where_ref, todo, x_in, h1, h2, h3, inc, res):
    listed = list_ref.shape[0]
    n_lanes = group * LANES
    chunks = nf // SUB
    halves = slots.shape[1]
    cap = 2 * halves // size
    x_in[nf:nf + SUB] = bias_ones(SUB, n_lanes)
    for h in (h1, h2, h3):
        h[h.shape[0] - 16:] = bias_ones(16, n_lanes).astype(jnp.bfloat16)
    res[...] = jnp.zeros_like(res)

    def clear(i, _):
        for j in range(SUB):
            where_ref[i * SUB + j] = size * cap
        return 0

    lax.fori_loop(0, cells // SUB, clear, 0)

    def note(i, _):
        for j in range(SUB):
            e = i * SUB + j
            entry = list_ref[e]
            where_ref[jnp.where(entry >= 0, entry, cells)] = (
                lax.rem(e, size) * cap + e // size)
        return 0

    lax.fori_loop(0, listed // SUB, note, 0)

    def pick(k, n):
        have = count_ref[k, 0, 0]
        for s in range(cap):
            todo[n] = k * cap + s
            n = n + jnp.where(s * size + k < have, 1, 0)
        return n

    count = lax.fori_loop(0, size, pick, 0)

    def run(g, _):
        base = g * group
        for i in range(group):
            slot = jnp.where(base + i < count, todo[base + i], 0)
            for c in range(chunks):
                tile = slots[c, slot // 2].astype(jnp.float32)
                x_in[c * SUB:(c + 1) * SUB, i * LANES:(i + 1) * LANES] = jnp.where(
                    lax.rem(slot, 2) == 0, tile[:SUB], tile[SUB:])
        inc[...] = network(x_in[...].astype(jnp.bfloat16), w1, w2, w3, w4, h1, h2, h3)
        for i in range(group):
            slot = jnp.where(base + i < count, todo[base + i], size * cap)
            for c in range(chunks):
                res[c, slot] = inc[c * SUB:(c + 1) * SUB, i * LANES:(i + 1) * LANES] - rest[
                    c * SUB:(c + 1) * SUB]
        return 0

    lax.fori_loop(0, (count + group - 1) // group, run, 0)
    for c in range(chunks):
        for p in range(halves):
            pair = jnp.concatenate([res[c, 2 * p], res[c, 2 * p + 1]], axis=0)
            ret_ref[c, p] = pair.astype(jnp.bfloat16)


def diffuse_kernel(nf, cx, cy, d_ref, where_ref, owner_ref, q_hbm, ret_hbm, rest_ref, out_hbm, act_out,
                   u_ref, new_ref, ret, got_ret, res, part, got, act_send, act_recv,
                   xs, xr, ys, yr, zs, zr, send_sem, recv_sem,
                   team_send, team_recv, in_sem, out_sem, ret_sem):
    grid = Grid(cx, cy)
    chunks = nf // SUB
    team = Team()
    pairs = ret.shape[2]
    cap = 2 * pairs
    own = pltpu.make_async_copy(ret_hbm, ret, ret_sem)
    own.start()
    loads = []
    for c in range(chunks):
        loads.append(pltpu.make_async_copy(
            q_hbm.at[pl.ds(c * SUB, SUB)],
            u_ref.at[pl.ds(c * SUB, SUB), pl.ds(1, cx), pl.ds(SUB, cy)], in_sem.at[c]))
        loads[-1].start()
    near = neighbours()
    groups = [peers(a) for a in AXES[::-1]]
    members = [team.member(team.size - k) for k in range(team.size)]
    enter([to for g in groups for to in g] + members[1:])
    halo = Halo(grid, SUB, near, xs, xr, ys, yr, zs, zr, send_sem, recv_sem)
    lane = lane_ids()
    u2 = u_ref.reshape(nf * grid.px * grid.py, LANES)
    own.wait()
    backs = [[remote(ret.at[c, k], got_ret.at[c, k], team_send.at[c, k], team_recv.at[c, k],
                     members[k]) for k in range(1, team.size)] for c in range(chunks)]
    for copies in backs:
        for copy in copies:
            copy.start()

    def hops(phase):
        return [remote(part.at[phase], got.at[phase, k], act_send.at[phase, k],
                       act_recv.at[phase, k], to)
                for k, to in enumerate(groups[phase])]

    def gather(phase):
        for h in hops(phase):
            h.wait_recv()
        total = part[phase]
        for k in range(len(groups[phase])):
            total = total + got[phase, k]
        return total

    flat = lax.broadcasted_iota(jnp.int32, (SUB, LANES), 0) * LANES + lane

    def heat():
        total = jnp.zeros((SUB, LANES), jnp.float32)
        for e in range(owner_ref.shape[0]):
            r = res[0, (e % team.size) * cap + e // team.size][0:1]
            warm = jnp.sum(r * r, axis=1, keepdims=True) * (1.0 / (8.0 * LANES))
            total = total + jnp.where(flat == owner_ref[e], warm, 0.0)
        return total

    for c in range(chunks):
        loads[c].wait()
        res[c, team.size * cap] = jnp.zeros((SUB, LANES), jnp.float32)
        rest = rest_ref[c * SUB:(c + 1) * SUB]
        for copy in backs[c]:
            copy.wait_recv()
        for k in range(team.size):
            for p in range(pairs):
                tile = (got_ret if k else ret)[c, k, p].astype(jnp.float32)
                res[c, k * cap + 2 * p] = tile[:SUB] + rest
                res[c, k * cap + 2 * p + 1] = tile[SUB:] + rest

        def add(x, _):
            for y in range(cy):
                t = res[c, where_ref[x * cy + y]]
                at = pl.ds(grid.row(c * SUB, x, y), SUB, stride=grid.px * grid.py)
                u2[at, :] = u2[at, :] + t
            return 0

        lax.fori_loop(0, cx, add, 0)
        halo.load_z(c, u2, c * SUB)
        halo.send(c, u2, c * SUB)
        if c == 0:
            part[0] = heat()
            for h in hops(0):
                h.start()
    stores = []
    for c in range(chunks):
        if c < len(groups) - 1:
            part[c + 1] = gather(c)
            for h in hops(c + 1):
                h.start()
        first = c * SUB
        halo.receive(c, u2, first)

        def body(x, _):
            zrow = halo.z_row(c, x)
            for f in range(SUB):
                rate = d_ref[first + f]
                for g in range(grid.groups):
                    row = grid.tile(first + f, x, g)
                    t = u2[pl.ds(row, SUB), :]
                    za, zb = halo.z_near(t, zrow, f * grid.groups + g)
                    s = u2[pl.ds(row + grid.py, SUB), :] + u2[pl.ds(row - grid.py, SUB), :]
                    s = s + (u2[pl.ds(row + 1, SUB), :] + u2[pl.ds(row - 1, SUB), :])
                    s = s + (za + zb)
                    new_ref[first + f, x, pl.ds(g * SUB, SUB)] = t + rate * (s - 6.0 * t)
            return 0

        lax.fori_loop(0, cx, body, 0)
        chunk = pl.ds(first, SUB)
        stores.append(pltpu.make_async_copy(new_ref.at[chunk], out_hbm.at[chunk], out_sem.at[c]))
        stores[-1].start()
    done = min(chunks, len(groups) - 1)
    for phase in range(done, len(groups) - 1):
        part[phase + 1] = gather(phase)
        for h in hops(phase + 1):
            h.start()
    total = gather(len(groups) - 1)
    me = (lax.axis_index("gx") * lax.axis_size("gy") + lax.axis_index("gy")) * lax.axis_size(
        "gz") + lax.axis_index("gz")
    act_out[0] = jnp.sum(jnp.where(flat == me, total, 0.0))
    for phase in range(len(groups)):
        for h in hops(phase):
            h.wait_send()
    for copies in backs:
        for copy in copies:
            copy.wait_send()
    for c in range(chunks):
        halo.finish(c)
    for copy in stores:
        copy.wait()


def halo_scratch(slots, cx, cy):
    return [
        pltpu.VMEM((slots, 2, SUB, cy, LANES), jnp.bfloat16),
        pltpu.VMEM((slots, 2, SUB, cy, LANES), jnp.bfloat16),
        pltpu.VMEM((slots, 2, SUB, cx, LANES), jnp.float32),
        pltpu.VMEM((slots, 2, SUB, cx, LANES), jnp.float32),
        pltpu.VMEM((slots, cx, SUB, LANES), jnp.float32),
        pltpu.VMEM((slots, 2, cx, SUB, LANES), jnp.float32),
        pltpu.SemaphoreType.DMA((slots, 6)),
        pltpu.SemaphoreType.DMA((slots, 6)),
    ]


def spec(space, n=1):
    return [pl.BlockSpec(memory_space=space)] * n


def local(fields, velocity, diffusivity, weight_in, bias_in, weight_mid, bias_mid,
          weight_low, bias_low, weight_out, bias_out, react_list, owner_table):
    nf, cx, cy, cz = fields.shape
    chunks = nf // SUB
    cells = cx * cy
    padded = (cx + 2, cy + 2 * SUB, cz)
    slots = 3 * chunks
    dma = pltpu.SemaphoreType.DMA
    f32, bf16 = jnp.float32, jnp.bfloat16
    listed = react_list.shape[1]
    team = Team()
    size, cap = team.size, team.slots(listed)
    traffic = (chunks, size, cap // 2, 2 * SUB, LANES)
    h = (weight_in.shape[1], weight_mid.shape[1], weight_low.shape[1])
    wide = up(h[0], LANES)
    bias_wide = up(h[1], LANES) + up(h[2], LANES) + up(nf, LANES)
    w_shapes = [(wide, 32), (h[1], h[0] + 16), (h[2], h[1] + 16), (nf, h[2] + 16)]

    flowed, sent, counts, rest, w1, w2, w3, w4 = pl.pallas_call(
        functools.partial(flow_kernel, nf, cx, cy),
        out_shape=(jax.ShapeDtypeStruct(fields.shape, f32),
                   jax.ShapeDtypeStruct(traffic, bf16),
                   jax.ShapeDtypeStruct((size, 1, LANES), jnp.int32),
                   jax.ShapeDtypeStruct((nf, LANES), f32))
        + tuple(jax.ShapeDtypeStruct(w, bf16) for w in w_shapes),
        in_specs=spec(pltpu.HBM, 11),
        out_specs=tuple(spec(pl.ANY, 8)),
        scratch_shapes=[pltpu.SMEM((1, listed), jnp.int32)]
        + [pltpu.VMEM((nf,) + padded, f32)] * 3 + [
            pltpu.VMEM((3,) + padded, f32),
            pltpu.VMEM((nf, cx, cy, cz), f32),
            pltpu.VMEM((6, cx, cy // SUB, SUB, cz), f32),
            pltpu.VMEM(traffic, bf16),
            pltpu.VMEM(traffic, bf16),
            pltpu.VMEM((1, LANES), jnp.int32),
            pltpu.VMEM((size, 1, LANES), jnp.int32),
            pltpu.VMEM((nf, h[0]), bf16),
            pltpu.VMEM((h[1], h[0]), bf16),
            pltpu.VMEM((h[2], h[1]), bf16),
            pltpu.VMEM((nf, h[2]), bf16),
            pltpu.VMEM((h[0],), f32),
            pltpu.VMEM((h[1],), f32),
            pltpu.VMEM((h[2],), f32),
            pltpu.VMEM((nf,), f32),
            pltpu.VMEM((32, wide), f32),
            pltpu.VMEM((32, bias_wide), f32),
            pltpu.VMEM((bias_wide, 32), bf16),
        ] + [pltpu.VMEM(w, bf16) for w in w_shapes] + [
            pltpu.VMEM((h[0] + 16, LANES), bf16),
            pltpu.VMEM((h[1] + 16, LANES), bf16),
            pltpu.VMEM((h[2] + 16, LANES), bf16),
            pltpu.VMEM((nf, LANES), f32),
            pltpu.VMEM((2, cy, cz), f32),
            pltpu.VMEM((2, cx, cz), f32),
            pltpu.VMEM((2, cx, SUB, cz), f32),
            pltpu.VMEM((2, cx, cz), f32),
            pltpu.VMEM((cx, SUB, cz), f32),
        ] + halo_scratch(slots, cx, cy) + [
            dma((6,)), dma((6,)), dma((chunks + 1,)), dma((chunks,)),
            dma((chunks + 1, size)), dma((chunks + 1, size)), dma((9,)), dma((5,)), dma((2,))],
        compiler_params=pltpu.CompilerParams(
            collective_id=0, has_side_effects=True, vmem_limit_bytes=48 * MIB),
        name="flow",
    )(*[pltpu.with_memory_space_constraint(a, pltpu.HBM) for a in (
        react_list, fields, velocity, weight_in, weight_mid.T, weight_low.T, weight_out.T,
        bias_in, bias_mid, bias_low, bias_out)])

    group = 4
    n_lanes = group * LANES
    halves = size * cap // 2
    ret, where = pl.pallas_call(
        functools.partial(chem_kernel, nf, cells, group, size),
        out_shape=(jax.ShapeDtypeStruct((chunks, halves, 2 * SUB, LANES), bf16),
                   jax.ShapeDtypeStruct((cells + SUB,), jnp.int32)),
        in_specs=spec(pltpu.SMEM, 2) + spec(pltpu.VMEM, 6),
        out_specs=(spec(pltpu.VMEM)[0], spec(pltpu.SMEM)[0]),
        scratch_shapes=[
            pltpu.SMEM((size * cap + group,), jnp.int32),
            pltpu.VMEM((nf + SUB, n_lanes), f32),
            pltpu.VMEM((h[0] + 16, n_lanes), bf16),
            pltpu.VMEM((h[1] + 16, n_lanes), bf16),
            pltpu.VMEM((h[2] + 16, n_lanes), bf16),
            pltpu.VMEM((nf, n_lanes), f32),
            pltpu.VMEM((chunks, size * cap + 1, SUB, LANES), f32),
        ],
        compiler_params=pltpu.CompilerParams(vmem_limit_bytes=40 * MIB),
        name="chem",
    )(react_list[0], counts, sent.reshape(chunks, halves, 2 * SUB, LANES), rest,
      w1, w2, w3, w4)

    most = max(lax.axis_size(a) for a in AXES) - 1
    updated, mine = pl.pallas_call(
        functools.partial(diffuse_kernel, nf, cx, cy),
        out_shape=(jax.ShapeDtypeStruct(fields.shape, f32),
                   jax.ShapeDtypeStruct((1,), f32)),
        in_specs=spec(pltpu.SMEM, 3) + spec(pl.ANY, 2) + spec(pltpu.VMEM),
        out_specs=(spec(pl.ANY)[0], spec(pltpu.SMEM)[0]),
        scratch_shapes=[
            pltpu.VMEM((nf,) + padded, f32),
            pltpu.VMEM((nf, cx, cy, cz), f32),
            pltpu.VMEM(traffic, bf16),
            pltpu.VMEM(traffic, bf16),
            pltpu.VMEM((chunks, size * cap + 1, SUB, LANES), f32),
            pltpu.VMEM((len(AXES), SUB, LANES), f32),
            pltpu.VMEM((len(AXES), most, SUB, LANES), f32),
            dma((len(AXES), most)),
            dma((len(AXES), most)),
        ] + halo_scratch(chunks, cx, cy) + [
            dma((chunks, size)), dma((chunks, size)), dma((chunks,)), dma((chunks,)), dma],
        compiler_params=pltpu.CompilerParams(
            collective_id=1, has_side_effects=True, vmem_limit_bytes=48 * MIB),
        name="diffuse",
    )(diffusivity, where, owner_table[0], flowed, ret.reshape(traffic), rest)
    return updated, mine


def solution(mesh):
    return jax.shard_map(
        local,
        mesh=mesh,
        in_specs=(P(None, *AXES), P(None, *AXES)) + (P(),) * 9
        + (P(AXES, None), P(AXES, None)),
        out_specs=(P(None, *AXES), P(AXES)),
        check_vma=False,
    )
```

```python
import functools

import jax
import jax.numpy as jnp
from jax import lax
from jax.experimental import pallas as pl
from jax.experimental.pallas import tpu as pltpu
from jax.sharding import PartitionSpec as P

AXES = ("gx", "gy", "gz")
MESH = pl.DeviceIdType.MESH
SUB = 8
LANES = 128
MIB = 1024 * 1024


def neighbours():
    ids = {a: lax.axis_index(a) for a in AXES}
    out = []
    for a in AXES:
        n = lax.axis_size(a)
        up = dict(ids)
        up[a] = lax.rem(ids[a] + 1, n)
        down = dict(ids)
        down[a] = lax.rem(ids[a] + n - 1, n)
        out.append((tuple(up[b] for b in AXES), tuple(down[b] for b in AXES)))
    return out


def greet(targets):
    barrier = pltpu.get_barrier_semaphore()
    for to in targets:
        pl.semaphore_signal(barrier, inc=1, device_id=to, device_id_type=MESH)


def met(targets):
    pl.semaphore_wait(pltpu.get_barrier_semaphore(), len(targets))


def peers(axis):
    ids = {a: lax.axis_index(a) for a in AXES}
    n = lax.axis_size(axis)
    out = []
    for k in range(1, n):
        to = dict(ids)
        to[axis] = lax.rem(ids[axis] + k, n)
        out.append(tuple(to[b] for b in AXES))
    return out


def remote(src, dst, send, recv, to):
    return pltpu.make_async_remote_copy(
        src_ref=src, dst_ref=dst, send_sem=send, recv_sem=recv,
        device_id=to, device_id_type=MESH)


def lane_ids():
    return lax.broadcasted_iota(jnp.int32, (SUB, LANES), 1)


def odd_tiles(n):
    return n if n // SUB % 2 else n + SUB


def padded(cx, cy):
    return cx + 2 + (cx + 1) % 2, odd_tiles(cy + 2 * SUB), LANES


class Grid:
    def __init__(self, cx, cy):
        self.cx, self.cy = cx, cy
        self.px, self.py, _ = padded(cx, cy)
        self.groups = cy // SUB

    def row(self, f, x, y=0):
        return (f * self.px + x + 1) * self.py + SUB + y

    def tile(self, f, x, g):
        r = (f * self.px + x + 1) * self.py + SUB + g * SUB
        return r if isinstance(r, int) else pl.multiple_of(r, SUB)


class Halo:
    def __init__(self, grid, width, near, xs, xr, ys, yr, zs, zr, send_sem, recv_sem):
        self.grid, self.width, self.near = grid, width, near
        self.xs, self.xr, self.ys, self.yr = xs, xr, ys, yr
        self.zs, self.zr, self.send_sem, self.recv_sem = zs, zr, send_sem, recv_sem
        lane = lane_ids()
        self.first, self.last = lane == 0, lane == LANES - 1
        self.even = lax.rem(lane, 2) == 0
        self.pair = lax.rem(lane + 1, LANES) // 2

    def copies(self, slot, first=0, last=6):
        (xu, xd), (yu, yd), (zu, zd) = self.near
        plan = [
            (self.xs.at[slot, 1], self.xr.at[slot, 0], xu),
            (self.xs.at[slot, 0], self.xr.at[slot, 1], xd),
            (self.ys.at[slot, 1], self.yr.at[slot, 0], yu),
            (self.ys.at[slot, 0], self.yr.at[slot, 1], yd),
            (self.zs.at[slot], self.zr.at[slot, 0], zu),
        ]
        if lax.axis_size("gz") > 2:
            plan.append((self.zs.at[slot], self.zr.at[slot, 1], zd))
        return [
            remote(s, d, self.send_sem.at[slot, i], self.recv_sem.at[slot, i], to)
            for i, (s, d, to) in enumerate(plan) if first <= i < last
        ]

    def pack_z(self, face, t, k):
        return jnp.where(self.pair == k, pltpu.roll(t, 2 * k, 1) if k else t, face)

    def z_row(self, slot, x):
        if lax.axis_size("gz") > 2:
            return jnp.where(self.even, self.zr[slot, 1, x], self.zr[slot, 0, x])
        return self.zr[slot, 0, x]

    def z_near(self, t, zrow, k):
        r = pltpu.roll(zrow, LANES - 2 * k, 1) if k else zrow
        after = pltpu.roll(jnp.where(self.first, r, t), LANES - 1, 1)
        before = pltpu.roll(jnp.where(self.last, r, t), 1, 1)
        return after, before

    def pack_x(self, slot, u, base):
        grid = self.grid
        for f in range(self.width):
            for side, x in ((0, 0), (1, grid.cx - 1)):
                self.xs[slot, side, f] = u[
                    pl.ds(grid.tile(base + f, x, 0), grid.cy), :].astype(jnp.bfloat16)

    def send_x(self, slot):
        for c in self.copies(slot, 0, 2):
            c.start()

    def send_yz(self, slot, u, base):
        grid = self.grid
        for f in range(self.width):
            for side, y in ((0, 0), (1, grid.cy - 1)):
                self.ys[slot, side, f] = u[
                    pl.ds(grid.row(base + f, 0, y), grid.cx, stride=grid.py), :]
        for c in self.copies(slot, 2):
            c.start()

    def load_z(self, slot, u, base):
        grid = self.grid

        def body(i, _):
            for x in [i]:
                face = jnp.zeros((SUB, LANES), jnp.float32)
                for g in range(grid.groups):
                    for f in range(self.width):
                        t = u[pl.ds(grid.tile(base + f, x, g), SUB), :]
                        face = self.pack_z(face, t, f * grid.groups + g)
                self.zs[slot, x] = face
            return 0

        lax.fori_loop(0, grid.cx, body, 0)

    def receive(self, slot, u, base):
        grid = self.grid
        for c in self.copies(slot):
            c.wait_recv()
        for f in range(self.width):
            for side, x in ((0, -1), (1, grid.cx)):
                u[pl.ds(grid.tile(base + f, x, 0), grid.cy), :] = self.xr[
                    slot, side, f].astype(jnp.float32)
            for side, y in ((0, -1), (1, grid.cy)):
                u[pl.ds(grid.row(base + f, 0, y), grid.cx, stride=grid.py), :] = self.yr[
                    slot, side, f]

    def finish(self, slot):
        for c in self.copies(slot):
            c.wait_send()


class Team:
    def __init__(self):
        self.nx, self.ny, self.nz = (lax.axis_size(a) for a in AXES)
        self.span = 2 if self.ny % 2 == 0 else self.ny
        self.size = self.nx * self.span * self.nz

    def slots(self, listed):
        return 2 * ((listed + 2 * self.size - 1) // (2 * self.size))

    def place(self):
        i, j, k = (lax.axis_index(a) for a in AXES)
        return (i * self.span + lax.rem(j, self.span)) * self.nz + k

    def member(self, step):
        m = lax.rem(self.place() + step, self.size)
        i = m // (self.span * self.nz)
        j = lax.rem(m // self.nz, self.span)
        j = j + (lax.axis_index("gy") // self.span) * self.span
        return (i, j, lax.rem(m, self.nz))


def bias_rows(dst, row, lane, bias, scale):
    n = bias.shape[0]
    rest = bias[...].reshape(1, n) * scale
    for i in range(3):
        part = rest.astype(jnp.bfloat16).astype(jnp.float32)
        rest = rest - part
        dst[row + i:row + i + 1, lane:lane + n] = part


def turned(dst, src):
    for j in range(0, src.shape[1], LANES):
        dst[j:j + LANES] = src[:, j:j + LANES].T.astype(jnp.bfloat16)


def widen(dst, src, scale, cols, first):
    rows, k = src.shape
    step = 16 if rows % 16 == 0 else rows

    def body(j, _):
        at = pl.ds(pl.multiple_of(j * step, step), step)
        dst[at, pl.ds(0, k)] = src[at, :] * jnp.bfloat16(scale)
        dst[at, pl.ds(k, 16)] = cols[pl.ds(pl.multiple_of(first + j * step, 8), step),
                                     pl.ds(0, 16)]
        return 0

    lax.fori_loop(0, rows // step, body, 0)


def up(n, m):
    return (n + m - 1) // m * m


def flow_kernel(nf, cx, cy, list_hbm, q_hbm, v_hbm, wi_hbm, wm_hbm, wl_hbm, wo_hbm,
                b1_hbm, b2_hbm, b3_hbm, b4_hbm,
                out_hbm, rv, cr, where_ref, rest, w1, w2, w3, w4,
                list_ref, u0, u1, u2, w_ref, flow_ref, coef, sd, cs,
                wi, wm, wl, wo, b1, b2, b3, b4, t1, t2, cols, h1, h2, h3,
                vx, vy, vz, vys, vzs, xs, xr, ys, yr, zs, zr,
                send_sem, recv_sem, vs_sem, vr_sem, in_sem, out_sem,
                team_send, team_recv, w_in, tally_ref, tally_sem):
    grid = Grid(cx, cy)
    chunks = nf // SUB
    cells = cx * cy
    team = Team()
    listed = list_ref.shape[1]
    def fetch(c, kind, x, n):
        return pltpu.make_async_copy(
            q_hbm.at[pl.ds(c * SUB, SUB), pl.ds(x, n)],
            u0.at[pl.ds(c * SUB, SUB), pl.ds(1 + x, n), pl.ds(SUB, cy)], in_sem.at[c, kind])

    faces = [[fetch(c, 0, 0, 1), fetch(c, 1, cx - 1, 1)] for c in range(chunks)]
    inner = [fetch(c, 2, 1, cx - 2) for c in range(chunks)]
    v_load = pltpu.make_async_copy(
        v_hbm, w_ref.at[:, pl.ds(1, cx), pl.ds(SUB, cy)], in_sem.at[0, 3])
    w_loads = [pltpu.make_async_copy(src, dst, w_in.at[i]) for i, (src, dst) in enumerate((
        (wi_hbm, wi), (b1_hbm, b1), (b2_hbm, b2), (b3_hbm, b3), (b4_hbm, b4),
        (wo_hbm, wo), (list_hbm, list_ref), (wl_hbm, wl), (wm_hbm, wm)))]
    for copy in sum(faces, []) + [v_load] + inner:
        copy.start()
    near = neighbours()
    (xu, xd), (yu, yd), (zu, zd) = near
    halo = Halo(grid, SUB, near, xs, xr, ys, yr, zs, zr, send_sem, recv_sem)
    rows = nf * grid.px * grid.py
    us = [u.reshape(rows, LANES) for u in (u0, u1, u2)]
    vv = w_ref.reshape(3 * grid.px * grid.py, LANES)
    members = [team.member(k) for k in range(team.size)]
    known = [to for pair in near for to in pair] + members[1:]
    greet(known)
    for c in range(chunks):
        for copy in faces[c]:
            copy.wait()
        halo.pack_x(c, us[0], c * SUB)
        if c == 0:
            met(known)
        halo.send_x(c)
    v_load.wait()
    for side, y in ((0, 0), (1, cy - 1)):
        vys[side] = vv[pl.ds(grid.row(1, 0, y), cx, stride=grid.py), :]

    def pack_v(x, _):
        face = jnp.zeros((SUB, LANES), jnp.float32)
        for g in range(grid.groups):
            face = halo.pack_z(face, vv[pl.ds(grid.tile(2, x, g), SUB), :], g)
        vzs[x] = face
        return 0

    lax.fori_loop(0, cx, pack_v, 0)
    plan = [
        (w_ref.at[0, cx, pl.ds(SUB, cy)], vx.at[0], xu),
        (w_ref.at[0, 1, pl.ds(SUB, cy)], vx.at[1], xd),
        (vys.at[1], vy.at[0], yu),
        (vys.at[0], vy.at[1], yd),
        (vzs, vz.at[0], zu),
    ]
    if lax.axis_size("gz") > 2:
        plan.append((vzs, vz.at[1], zd))
    v_copies = [remote(s, d, vs_sem.at[i], vr_sem.at[i], to)
                for i, (s, d, to) in enumerate(plan)]
    for copy in v_copies:
        copy.start()
    for copy in inner:
        copy.wait()
    for copy in w_loads:
        copy.start()
    for c in range(chunks):
        halo.load_z(c, us[0], c * SUB)
        halo.send_yz(c, us[0], c * SUB)

    for copy in w_loads:
        copy.wait()
    count = lax.fori_loop(
        0, listed, lambda i, n: n + jnp.where(list_ref[0, i] >= 0, 1, 0), 0)
    cs[...] = jnp.full((1, LANES), count, jnp.int32)
    cr[0] = cs[...]
    counts = [remote(cs, cr.at[k], team_send.at[chunks, k], team_recv.at[chunks, k], members[k])
              for k in range(1, team.size)]
    for copy in counts:
        copy.start()

    t1[...] = jnp.zeros_like(t1)
    t2[...] = jnp.zeros_like(t2)
    n2, n3 = up(w2.shape[0], LANES), up(w3.shape[0], LANES)
    t1[0:nf, 0:wi.shape[1]] = wi[...].astype(jnp.float32) * 0.5
    bias_rows(t1, nf, 0, b1, 0.5)
    bias_rows(t2, 0, 0, b2, 0.5)
    bias_rows(t2, 0, n2, b3, 0.5)
    bias_rows(t2, 0, n2 + n3, b4, 1.0)
    turned(w1, t1)
    turned(cols, t2)
    widen(w2, wm, 0.5, cols, 0)
    widen(w3, wl, 0.5, cols, n2)
    widen(w4, wo, 1.0, cols, n2 + n3)
    for h in (h1, h2, h3):
        h[h.shape[0] - 16:] = bias_ones(16, LANES).astype(jnp.bfloat16)
    origin = jnp.concatenate(
        [jnp.zeros((nf, LANES), jnp.float32), bias_ones(w1.shape[1] - nf, LANES)], axis=0)
    rest[...] = network(origin.astype(jnp.bfloat16), w1, w2, w3, w4, h1, h2, h3)

    for copy in v_copies:
        copy.wait_recv()
    for side, x in ((0, -1), (1, cx)):
        vv[pl.ds(grid.tile(0, x, 0), cy), :] = vx[side]
    for side, y in ((0, -1), (1, cy)):
        vv[pl.ds(grid.row(1, 0, y), cx, stride=grid.py), :] = vy[side]

    def make_coef(x, _):
        if lax.axis_size("gz") > 2:
            zrow = jnp.where(halo.even, vz[1, x], vz[0, x])
        else:
            zrow = vz[0, x]
        for g in range(grid.groups):
            r0 = grid.tile(0, x, g)
            r1 = grid.tile(1, x, g)
            after, before = halo.z_near(vv[pl.ds(grid.tile(2, x, g), SUB), :], zrow, g)
            values = (
                0.05 - 0.5 * vv[pl.ds(r0 + grid.py, SUB), :],
                0.05 + 0.5 * vv[pl.ds(r0 - grid.py, SUB), :],
                0.05 - 0.5 * vv[pl.ds(r1 + 1, SUB), :],
                0.05 + 0.5 * vv[pl.ds(r1 - 1, SUB), :],
                0.05 - 0.5 * after,
                0.05 + 0.5 * before,
            )
            for i, value in enumerate(values):
                coef[i, x, g] = value
        return 0

    lax.fori_loop(0, cx, make_coef, 0)

    room = flow_ref.shape[1]
    cap = 2 * sd.shape[2]
    for copy in counts:
        copy.wait_recv()
    tally = pltpu.make_async_copy(cr, tally_ref, tally_sem)
    tally.start()
    tally.wait()
    me = team.place()
    ahead = lax.fori_loop(1, team.size, lambda k, n: n + jnp.where(
        k <= me, tally_ref[k, 0, 0], 0), 0)
    shift = lax.rem(ahead + team.size - me, team.size)
    home = lax.broadcasted_iota(jnp.int32, where_ref.shape, 0) * LANES + (
        lax.broadcasted_iota(jnp.int32, where_ref.shape, 1))
    table = jnp.where(home == cells, shift, team.size * cap)
    for e in range(listed):
        slot = lax.rem(shift + e, team.size) * cap + e // team.size
        table = jnp.where(home == list_ref[0, e], slot, table)
    where_ref[...] = table
    flow2 = flow_ref.reshape(nf * room, LANES)
    sends, stores = [], []

    def block(c, s, k):
        e = s * team.size + lax.rem(k + team.size - shift, team.size)
        b = jnp.maximum(list_ref[0, jnp.minimum(e, listed - 1)], 0)
        return flow2[pl.ds(c * SUB * room + b, SUB, stride=room), :]

    def dispatch(c):
        for k in range(team.size):
            dst = sd if k else rv
            for p in range(sd.shape[2]):
                pair = [block(c, 2 * p + h, k) for h in range(2)]
                dst[c, k, p] = jnp.concatenate(pair, axis=0).astype(jnp.bfloat16)
        for k in range(1, team.size):
            sends.append(remote(sd.at[c, k], rv.at[c, k], team_send.at[c, k],
                                team_recv.at[c, k], members[k]))
            sends[-1].start()

    for stage in range(3):
        weight = (1.0 / 3.0, 0.5, 1.0)[stage]
        u = us[stage]
        for c in range(chunks):
            slot = stage * chunks + c
            first = c * SUB
            halo.receive(slot, u, first)

            def body(i, _):
                for x in [i]:
                    zrow = halo.z_row(slot, x)
                    face = jnp.zeros((SUB, LANES), jnp.float32)
                    for g in range(grid.groups):
                        ks = [coef[j, x, g] for j in range(6)]
                        for f in range(SUB):
                            k = f * grid.groups + g
                            row = grid.tile(first + f, x, g)
                            t = u[pl.ds(row, SUB), :]
                            za, zb = halo.z_near(t, zrow, k)
                            s = (ks[0] * u[pl.ds(row + grid.py, SUB), :]
                                 + ks[1] * u[pl.ds(row - grid.py, SUB), :])
                            s = s + (ks[2] * u[pl.ds(row + 1, SUB), :]
                                     + ks[3] * u[pl.ds(row - 1, SUB), :])
                            s = s + (ks[4] * za + ks[5] * zb)
                            q = t if stage == 0 else us[0][pl.ds(row, SUB), :]
                            r = q + weight * (s - 0.3 * t)
                            if stage == 2:
                                at = pl.multiple_of(x * cy + g * SUB, SUB)
                                flow_ref[first + f, pl.ds(at, SUB)] = r
                            else:
                                us[stage + 1][pl.ds(row, SUB), :] = r
                                face = halo.pack_z(face, r, k)
                    if stage < 2:
                        zs[slot + chunks, x] = face
                return 0

            lax.fori_loop(0, cx, body, 0)
            if stage < 2:
                halo.pack_x(slot + chunks, us[stage + 1], first)
                halo.send_x(slot + chunks)
                halo.send_yz(slot + chunks, us[stage + 1], first)
            else:
                dispatch(c)
                part = pl.ds(first, SUB)
                stores.append(pltpu.make_async_copy(
                    flow_ref.at[part, pl.ds(0, cells)], out_hbm.at[part], out_sem.at[c]))
                stores[-1].start()
    for copy in sends:
        copy.wait_recv()
    for copy in v_copies + counts + sends:
        copy.wait_send()
    for slot in range(3 * chunks):
        halo.finish(slot)
    for copy in stores:
        copy.wait()


def layer(w, src, dst, step):
    rows = dst.shape[0] - 16
    for m in range(0, rows, step):
        k = min(step, rows - m)
        h = jnp.dot(w[m:m + k], src, preferred_element_type=jnp.float32)
        dst[m:m + k] = (h + h * jnp.tanh(h)).astype(jnp.bfloat16)


def network(x, w1, w2, w3, w4, h1, h2, h3):
    layer(w1, x, h1, 400)
    layer(w2, h1[...], h2, 400)
    layer(w3, h2[...], h3, 400)
    return jnp.dot(w4[...], h3[...], preferred_element_type=jnp.float32)


def bias_ones(rows, lanes):
    return jnp.where(lax.broadcasted_iota(jnp.int32, (rows, lanes), 0) < 3, 1.0, 0.0)


def chem_kernel(nf, group, size, count_ref, slots, rest, w1, w2, w3,
                w4, ret_ref, todo, x_in, h1, h2, h3, inc, res):
    n_lanes = group * LANES
    chunks = nf // SUB
    halves = slots.shape[1]
    cap = 2 * halves // size
    x_in[nf:nf + SUB] = bias_ones(SUB, n_lanes)
    for h in (h1, h2, h3):
        h[h.shape[0] - 16:] = bias_ones(16, n_lanes).astype(jnp.bfloat16)
    res[...] = jnp.zeros_like(res)

    me = Team().place()

    def pick(m, carry):
        ahead, n = carry
        k = lax.rem(me + size - m, size)
        have = count_ref[k, 0, 0]
        first = lax.rem(k + 2 * size - lax.rem(ahead + size - m, size), size)
        for s in range(cap):
            todo[n] = k * cap + s
            n = n + jnp.where(s * size + first < have, 1, 0)
        return ahead + have, n

    count = lax.fori_loop(0, size, pick, (0, 0))[1]

    def run(g, _):
        base = g * group
        for i in range(group):
            slot = jnp.where(base + i < count, todo[base + i], 0)
            for c in range(chunks):
                tile = slots[c, slot // 2].astype(jnp.float32)
                x_in[c * SUB:(c + 1) * SUB, i * LANES:(i + 1) * LANES] = jnp.where(
                    lax.rem(slot, 2) == 0, tile[:SUB], tile[SUB:])
        inc[...] = network(x_in[...].astype(jnp.bfloat16), w1, w2, w3, w4, h1, h2, h3)
        for i in range(group):
            slot = jnp.where(base + i < count, todo[base + i], size * cap)
            for c in range(chunks):
                res[c, slot] = inc[c * SUB:(c + 1) * SUB, i * LANES:(i + 1) * LANES] - rest[
                    c * SUB:(c + 1) * SUB]
        return 0

    lax.fori_loop(0, (count + group - 1) // group, run, 0)
    for c in range(chunks):
        for p in range(halves):
            pair = jnp.concatenate([res[c, 2 * p], res[c, 2 * p + 1]], axis=0)
            ret_ref[c, p] = pair.astype(jnp.bfloat16)


def diffuse_kernel(nf, cx, cy, d_ref, where_ref, owner_ref, q_hbm, ret_hbm, rest_ref, out_hbm, act_out,
                   u_ref, old_ref, new_ref, ret, got_ret, res, part, got, act_send, act_recv,
                   xs, xr, ys, yr, zs, zr, send_sem, recv_sem,
                   team_send, team_recv, in_sem, out_sem, ret_sem):
    grid = Grid(cx, cy)
    chunks = nf // SUB
    team = Team()
    pairs = ret.shape[2]
    cells = cx * cy
    cap = 2 * pairs
    own = pltpu.make_async_copy(ret_hbm, ret, ret_sem)
    own.start()
    loads = []
    for c in range(chunks):
        loads.append(pltpu.make_async_copy(
            q_hbm.at[pl.ds(c * SUB, SUB)],
            old_ref.at[pl.ds(c * SUB, SUB), pl.ds(0, cells)], in_sem.at[c]))
        loads[-1].start()
    near = neighbours()
    groups = [peers(a) for a in AXES[::-1]]
    members = [team.member(team.size - k) for k in range(team.size)]
    known = [to for g in groups for to in g] + members[1:]
    greet(known)
    halo = Halo(grid, SUB, near, xs, xr, ys, yr, zs, zr, send_sem, recv_sem)
    lane = lane_ids()
    u2 = u_ref.reshape(nf * grid.px * grid.py, LANES)
    room = old_ref.shape[1]
    old2 = old_ref.reshape(nf * room, LANES)
    own.wait()
    met(known)
    backs = [[remote(ret.at[c, k], got_ret.at[c, k], team_send.at[c, k], team_recv.at[c, k],
                     members[k]) for k in range(1, team.size)] for c in range(chunks)]
    for copies in backs:
        for copy in copies:
            copy.start()

    def hops(phase):
        return [remote(part.at[phase], got.at[phase, k], act_send.at[phase, k],
                       act_recv.at[phase, k], to)
                for k, to in enumerate(groups[phase])]

    def gather(phase):
        for h in hops(phase):
            h.wait_recv()
        total = part[phase]
        for k in range(len(groups[phase])):
            total = total + got[phase, k]
        return total

    flat = lax.broadcasted_iota(jnp.int32, (SUB, LANES), 0) * LANES + lane

    listed = owner_ref.shape[0]

    def heat():
        total = jnp.zeros((SUB, LANES), jnp.float32)
        shift = where_ref[cells // LANES, cells % LANES]

        def body(k, total):
            first = lax.rem(k + team.size - shift, team.size)
            for s in range(cap):
                r = res[0, k * cap + s][0:1]
                warm = jnp.sum(r * r, axis=1, keepdims=True) * (1.0 / (8.0 * LANES))
                e = s * team.size + first
                owner = jnp.where(e < listed, owner_ref[jnp.minimum(e, listed - 1)], -1)
                total = total + jnp.where(flat == owner, warm, 0.0)
            return total

        total = lax.fori_loop(0, team.size, body, total)
        return total

    for c in range(chunks):
        loads[c].wait()
        res[c, team.size * cap] = jnp.zeros((SUB, LANES), jnp.float32)
        rest = rest_ref[c * SUB:(c + 1) * SUB]
        for copy in backs[c]:
            copy.wait_recv()
        for k in range(team.size):
            for p in range(pairs):
                tile = (got_ret if k else ret)[c, k, p].astype(jnp.float32)
                res[c, k * cap + 2 * p] = tile[:SUB] + rest
                res[c, k * cap + 2 * p + 1] = tile[SUB:] + rest

        def add(i, _):
            for x in [i]:
                line, lane0 = x * cy // LANES, lax.rem(x * cy, LANES)
                for y in range(cy):
                    b = x * cy + y
                    if LANES % cy:
                        line, lane0 = b // LANES, lax.rem(b, LANES) - y
                    t = res[c, where_ref[line, lane0 + y]]
                    old = old2[pl.ds(c * SUB * room + b, SUB, stride=room), :]
                    u2[pl.ds(grid.row(c * SUB, x, y), SUB, stride=grid.px * grid.py), :] = old + t
            return 0

        lax.fori_loop(0, cx, add, 0)
        halo.pack_x(c, u2, c * SUB)
        halo.send_x(c)
        halo.load_z(c, u2, c * SUB)
        halo.send_yz(c, u2, c * SUB)
        if c == 0:
            part[0] = heat()
            for h in hops(0):
                h.start()
    stores = []
    for c in range(chunks):
        if c < len(groups) - 1:
            part[c + 1] = gather(c)
            for h in hops(c + 1):
                h.start()
        first = c * SUB
        halo.receive(c, u2, first)

        def body(i, _):
            for x in [i]:
                zrow = halo.z_row(c, x)
                for f in range(SUB):
                    rate = d_ref[first + f]
                    for g in range(grid.groups):
                        row = grid.tile(first + f, x, g)
                        t = u2[pl.ds(row, SUB), :]
                        za, zb = halo.z_near(t, zrow, f * grid.groups + g)
                        s = u2[pl.ds(row + grid.py, SUB), :] + u2[pl.ds(row - grid.py, SUB), :]
                        s = s + (u2[pl.ds(row + 1, SUB), :] + u2[pl.ds(row - 1, SUB), :])
                        s = s + (za + zb)
                        new_ref[first + f, x, pl.ds(g * SUB, SUB)] = t + rate * (s - 6.0 * t)
            return 0

        lax.fori_loop(0, cx, body, 0)
        chunk = pl.ds(first, SUB)
        stores.append(pltpu.make_async_copy(new_ref.at[chunk], out_hbm.at[chunk], out_sem.at[c]))
        stores[-1].start()
    done = min(chunks, len(groups) - 1)
    for phase in range(done, len(groups) - 1):
        part[phase + 1] = gather(phase)
        for h in hops(phase + 1):
            h.start()
    total = gather(len(groups) - 1)
    me = (lax.axis_index("gx") * lax.axis_size("gy") + lax.axis_index("gy")) * lax.axis_size(
        "gz") + lax.axis_index("gz")
    act_out[0] = jnp.sum(jnp.where(flat == me, total, 0.0))
    for phase in range(len(groups)):
        for h in hops(phase):
            h.wait_send()
    for copies in backs:
        for copy in copies:
            copy.wait_send()
    for c in range(chunks):
        halo.finish(c)
    for copy in stores:
        copy.wait()


def halo_scratch(slots, cx, cy):
    return [
        pltpu.VMEM((slots, 2, SUB, cy, LANES), jnp.bfloat16),
        pltpu.VMEM((slots, 2, SUB, cy, LANES), jnp.bfloat16),
        pltpu.VMEM((slots, 2, SUB, cx, LANES), jnp.float32),
        pltpu.VMEM((slots, 2, SUB, cx, LANES), jnp.float32),
        pltpu.VMEM((slots, cx, SUB, LANES), jnp.float32),
        pltpu.VMEM((slots, 2, cx, SUB, LANES), jnp.float32),
        pltpu.SemaphoreType.DMA((slots, 6)),
        pltpu.SemaphoreType.DMA((slots, 6)),
    ]


def spec(space, n=1):
    return [pl.BlockSpec(memory_space=space)] * n


def local(fields, velocity, diffusivity, weight_in, bias_in, weight_mid, bias_mid,
          weight_low, bias_low, weight_out, bias_out, react_list, owner_table):
    nf, cx, cy, cz = fields.shape
    chunks = nf // SUB
    cells = cx * cy
    box = padded(cx, cy)
    room = odd_tiles(cells)
    slots = 3 * chunks
    dma = pltpu.SemaphoreType.DMA
    f32, bf16 = jnp.float32, jnp.bfloat16
    listed = react_list.shape[1]
    team = Team()
    size, cap = team.size, team.slots(listed)
    traffic = (chunks, size, cap // 2, 2 * SUB, LANES)
    h = (weight_in.shape[1], weight_mid.shape[1], weight_low.shape[1])
    wide = up(h[0], LANES)
    bias_wide = up(h[1], LANES) + up(h[2], LANES) + up(nf, LANES)
    w_shapes = [(wide, 32), (h[1], h[0] + 16), (h[2], h[1] + 16), (nf, h[2] + 16)]

    flowed, sent, counts, where, rest, w1, w2, w3, w4 = pl.pallas_call(
        functools.partial(flow_kernel, nf, cx, cy),
        out_shape=(jax.ShapeDtypeStruct((nf, cells, cz), f32),
                   jax.ShapeDtypeStruct(traffic, bf16),
                   jax.ShapeDtypeStruct((size, 1, LANES), jnp.int32),
                   jax.ShapeDtypeStruct((up(cells + 1, SUB * LANES) // LANES, LANES), jnp.int32),
                   jax.ShapeDtypeStruct((nf, LANES), f32))
        + tuple(jax.ShapeDtypeStruct(w, bf16) for w in w_shapes),
        in_specs=spec(pltpu.HBM, 11),
        out_specs=tuple(spec(pl.ANY) + spec(pltpu.VMEM, 8)),
        scratch_shapes=[pltpu.SMEM((1, listed), jnp.int32)]
        + [pltpu.VMEM((nf,) + box, f32)] * 3 + [
            pltpu.VMEM((3,) + box, f32),
            pltpu.VMEM((nf, room, cz), f32),
            pltpu.VMEM((6, cx, cy // SUB, SUB, cz), f32),
            pltpu.VMEM(traffic, bf16),
            pltpu.VMEM((1, LANES), jnp.int32),
            pltpu.VMEM((nf, h[0]), bf16),
            pltpu.VMEM((h[1], h[0]), bf16),
            pltpu.VMEM((h[2], h[1]), bf16),
            pltpu.VMEM((nf, h[2]), bf16),
            pltpu.VMEM((h[0],), f32),
            pltpu.VMEM((h[1],), f32),
            pltpu.VMEM((h[2],), f32),
            pltpu.VMEM((nf,), f32),
            pltpu.VMEM((32, wide), f32),
            pltpu.VMEM((32, bias_wide), f32),
            pltpu.VMEM((bias_wide, 32), bf16),
            pltpu.VMEM((h[0] + 16, LANES), bf16),
            pltpu.VMEM((h[1] + 16, LANES), bf16),
            pltpu.VMEM((h[2] + 16, LANES), bf16),
            pltpu.VMEM((2, cy, cz), f32),
            pltpu.VMEM((2, cx, cz), f32),
            pltpu.VMEM((2, cx, SUB, cz), f32),
            pltpu.VMEM((2, cx, cz), f32),
            pltpu.VMEM((cx, SUB, cz), f32),
        ] + halo_scratch(slots, cx, cy) + [
            dma((6,)), dma((6,)), dma((chunks, 4)), dma((chunks,)),
            dma((chunks + 1, size)), dma((chunks + 1, size)), dma((9,)),
            pltpu.SMEM((size, 1, LANES), jnp.int32), dma],
        compiler_params=pltpu.CompilerParams(
            collective_id=0, has_side_effects=True, vmem_limit_bytes=48 * MIB),
        name="flow",
    )(*[pltpu.with_memory_space_constraint(a, pltpu.HBM) for a in (
        react_list, fields, velocity, weight_in, weight_mid.T, weight_low.T, weight_out.T,
        bias_in, bias_mid, bias_low, bias_out)])

    group = 4
    n_lanes = group * LANES
    halves = size * cap // 2
    ret = pl.pallas_call(
        functools.partial(chem_kernel, nf, group, size),
        out_shape=jax.ShapeDtypeStruct((chunks, halves, 2 * SUB, LANES), bf16),
        in_specs=spec(pltpu.SMEM) + spec(pltpu.VMEM, 6),
        out_specs=spec(pltpu.VMEM)[0],
        scratch_shapes=[
            pltpu.SMEM((size * cap + group,), jnp.int32),
            pltpu.VMEM((nf + SUB, n_lanes), f32),
            pltpu.VMEM((h[0] + 16, n_lanes), bf16),
            pltpu.VMEM((h[1] + 16, n_lanes), bf16),
            pltpu.VMEM((h[2] + 16, n_lanes), bf16),
            pltpu.VMEM((nf, n_lanes), f32),
            pltpu.VMEM((chunks, size * cap + 1, SUB, LANES), f32),
        ],
        compiler_params=pltpu.CompilerParams(vmem_limit_bytes=40 * MIB),
        name="chem",
    )(counts, sent.reshape(chunks, halves, 2 * SUB, LANES), rest,
      w1, w2, w3, w4)

    most = max(lax.axis_size(a) for a in AXES) - 1
    updated, mine = pl.pallas_call(
        functools.partial(diffuse_kernel, nf, cx, cy),
        out_shape=(jax.ShapeDtypeStruct(fields.shape, f32),
                   jax.ShapeDtypeStruct((1,), f32)),
        in_specs=spec(pltpu.SMEM, 3) + spec(pl.ANY, 2) + spec(pltpu.VMEM),
        out_specs=(spec(pl.ANY)[0], spec(pltpu.SMEM)[0]),
        scratch_shapes=[
            pltpu.VMEM((nf,) + box, f32),
            pltpu.VMEM((nf, room, cz), f32),
            pltpu.VMEM((nf, cx, cy, cz), f32),
            pltpu.VMEM(traffic, bf16),
            pltpu.VMEM(traffic, bf16),
            pltpu.VMEM((chunks, size * cap + 1, SUB, LANES), f32),
            pltpu.VMEM((len(AXES), SUB, LANES), f32),
            pltpu.VMEM((len(AXES), most, SUB, LANES), f32),
            dma((len(AXES), most)),
            dma((len(AXES), most)),
        ] + halo_scratch(chunks, cx, cy) + [
            dma((chunks, size)), dma((chunks, size)), dma((chunks,)), dma((chunks,)), dma],
        compiler_params=pltpu.CompilerParams(
            collective_id=1, has_side_effects=True, vmem_limit_bytes=48 * MIB),
        name="diffuse",
    )(diffusivity, where, owner_table[0], flowed, ret.reshape(traffic), rest)
    return updated, mine


def solution(mesh):
    return jax.shard_map(
        local,
        mesh=mesh,
        in_specs=(P(None, *AXES), P(None, *AXES)) + (P(),) * 9
        + (P(AXES, None), P(AXES, None)),
        out_specs=(P(None, *AXES), P(AXES)),
        check_vma=False,
    )
```

```python
import functools

import jax
import jax.numpy as jnp
from jax import lax
from jax.experimental import pallas as pl
from jax.experimental.pallas import tpu as pltpu
from jax.sharding import PartitionSpec as P

AXES = ("gx", "gy", "gz")
MESH = pl.DeviceIdType.MESH
SUB = 8
LANES = 128
MIB = 1024 * 1024


def neighbours():
    ids = {a: lax.axis_index(a) for a in AXES}
    out = []
    for a in AXES:
        n = lax.axis_size(a)
        up = dict(ids)
        up[a] = lax.rem(ids[a] + 1, n)
        down = dict(ids)
        down[a] = lax.rem(ids[a] + n - 1, n)
        out.append((tuple(up[b] for b in AXES), tuple(down[b] for b in AXES)))
    return out


def greet(targets):
    barrier = pltpu.get_barrier_semaphore()
    for to in targets:
        pl.semaphore_signal(barrier, inc=1, device_id=to, device_id_type=MESH)


def met(targets):
    pl.semaphore_wait(pltpu.get_barrier_semaphore(), len(targets))


def peers(axis):
    ids = {a: lax.axis_index(a) for a in AXES}
    n = lax.axis_size(axis)
    out = []
    for k in range(1, n):
        to = dict(ids)
        to[axis] = lax.rem(ids[axis] + k, n)
        out.append(tuple(to[b] for b in AXES))
    return out


def remote(src, dst, send, recv, to):
    return pltpu.make_async_remote_copy(
        src_ref=src, dst_ref=dst, send_sem=send, recv_sem=recv,
        device_id=to, device_id_type=MESH)


def lane_ids():
    return lax.broadcasted_iota(jnp.int32, (SUB, LANES), 1)


def odd_tiles(n):
    return n if n // SUB % 2 else n + SUB


def padded(cx, cy):
    return cx + 2 + (cx + 1) % 2, odd_tiles(cy + 2 * SUB), LANES


class Grid:
    def __init__(self, cx, cy):
        self.cx, self.cy = cx, cy
        self.px, self.py, _ = padded(cx, cy)
        self.groups = cy // SUB

    def row(self, f, x, y=0):
        return (f * self.px + x + 1) * self.py + SUB + y

    def tile(self, f, x, g):
        r = (f * self.px + x + 1) * self.py + SUB + g * SUB
        return r if isinstance(r, int) else pl.multiple_of(r, SUB)


class Halo:
    def __init__(self, grid, width, near, xs, xr, ys, yr, zs, zr, send_sem, recv_sem):
        self.grid, self.width, self.near = grid, width, near
        self.xs, self.xr, self.ys, self.yr = xs, xr, ys, yr
        self.zs, self.zr, self.send_sem, self.recv_sem = zs, zr, send_sem, recv_sem
        lane = lane_ids()
        self.first, self.last = lane == 0, lane == LANES - 1
        self.even = lax.rem(lane, 2) == 0
        self.pair = lax.rem(lane + 1, LANES) // 2

    def copies(self, slot, first=0, last=6):
        (xu, xd), (yu, yd), (zu, zd) = self.near
        plan = [
            (self.xs.at[slot, 1], self.xr.at[slot, 0], xu),
            (self.xs.at[slot, 0], self.xr.at[slot, 1], xd),
            (self.ys.at[slot, 1], self.yr.at[slot, 0], yu),
            (self.ys.at[slot, 0], self.yr.at[slot, 1], yd),
            (self.zs.at[slot], self.zr.at[slot, 0], zu),
        ]
        if lax.axis_size("gz") > 2:
            plan.append((self.zs.at[slot], self.zr.at[slot, 1], zd))
        return [
            remote(s, d, self.send_sem.at[slot, i], self.recv_sem.at[slot, i], to)
            for i, (s, d, to) in enumerate(plan) if first <= i < last
        ]

    def pack_z(self, face, t, k):
        return jnp.where(self.pair == k, pltpu.roll(t, 2 * k, 1) if k else t, face)

    def z_row(self, slot, x):
        if lax.axis_size("gz") > 2:
            return jnp.where(self.even, self.zr[slot, 1, x], self.zr[slot, 0, x])
        return self.zr[slot, 0, x]

    def z_near(self, t, zrow, k):
        r = pltpu.roll(zrow, LANES - 2 * k, 1) if k else zrow
        after = pltpu.roll(jnp.where(self.first, r, t), LANES - 1, 1)
        before = pltpu.roll(jnp.where(self.last, r, t), 1, 1)
        return after, before

    def pack_x(self, slot, u, base):
        grid = self.grid
        for f in range(self.width):
            for side, x in ((0, 0), (1, grid.cx - 1)):
                self.xs[slot, side, f] = u[
                    pl.ds(grid.tile(base + f, x, 0), grid.cy), :].astype(jnp.bfloat16)

    def send_x(self, slot):
        for c in self.copies(slot, 0, 2):
            c.start()

    def send_yz(self, slot, u, base):
        grid = self.grid
        for f in range(self.width):
            for side, y in ((0, 0), (1, grid.cy - 1)):
                self.ys[slot, side, f] = u[
                    pl.ds(grid.row(base + f, 0, y), grid.cx, stride=grid.py), :]
        for c in self.copies(slot, 2):
            c.start()

    def load_z(self, slot, u, base):
        grid = self.grid

        def body(i, _):
            for x in [i]:
                face = jnp.zeros((SUB, LANES), jnp.float32)
                for g in range(grid.groups):
                    for f in range(self.width):
                        t = u[pl.ds(grid.tile(base + f, x, g), SUB), :]
                        face = self.pack_z(face, t, f * grid.groups + g)
                self.zs[slot, x] = face
            return 0

        lax.fori_loop(0, grid.cx, body, 0)

    def receive(self, slot, u, base):
        grid = self.grid
        for c in self.copies(slot):
            c.wait_recv()
        for f in range(self.width):
            for side, x in ((0, -1), (1, grid.cx)):
                u[pl.ds(grid.tile(base + f, x, 0), grid.cy), :] = self.xr[
                    slot, side, f].astype(jnp.float32)
            for side, y in ((0, -1), (1, grid.cy)):
                u[pl.ds(grid.row(base + f, 0, y), grid.cx, stride=grid.py), :] = self.yr[
                    slot, side, f]

    def finish(self, slot):
        for c in self.copies(slot):
            c.wait_send()


class Team:
    def __init__(self):
        self.nx, self.ny, self.nz = (lax.axis_size(a) for a in AXES)
        self.span = 2 if self.ny % 2 == 0 else self.ny
        self.size = self.nx * self.span * self.nz

    def slots(self, listed):
        return 2 * ((listed + 2 * self.size - 1) // (2 * self.size))

    def place(self):
        i, j, k = (lax.axis_index(a) for a in AXES)
        return (i * self.span + lax.rem(j, self.span)) * self.nz + k

    def member(self, step):
        m = lax.rem(self.place() + step, self.size)
        i = m // (self.span * self.nz)
        j = lax.rem(m // self.nz, self.span)
        j = j + (lax.axis_index("gy") // self.span) * self.span
        return (i, j, lax.rem(m, self.nz))


def bias_rows(dst, row, lane, bias, scale):
    n = bias.shape[0]
    rest = bias[...].reshape(1, n) * scale
    for i in range(3):
        part = rest.astype(jnp.bfloat16).astype(jnp.float32)
        rest = rest - part
        dst[row + i:row + i + 1, lane:lane + n] = part


def turned(dst, src):
    for j in range(0, src.shape[1], LANES):
        dst[j:j + LANES] = src[:, j:j + LANES].T.astype(jnp.bfloat16)


def widen(dst, src, scale, cols, first):
    rows, k = src.shape
    step = 16 if rows % 16 == 0 else rows

    def body(j, _):
        at = pl.ds(pl.multiple_of(j * step, step), step)
        dst[at, pl.ds(0, k)] = src[at, :] * jnp.bfloat16(scale)
        dst[at, pl.ds(k, 16)] = cols[pl.ds(pl.multiple_of(first + j * step, 8), step),
                                     pl.ds(0, 16)]
        return 0

    lax.fori_loop(0, rows // step, body, 0)


def up(n, m):
    return (n + m - 1) // m * m


def flow_kernel(nf, cx, cy, list_hbm, q_hbm, v_hbm, wi_hbm, wm_hbm, wl_hbm, wo_hbm,
                b1_hbm, b2_hbm, b3_hbm, b4_hbm,
                out_hbm, rv, cr, where_ref, rest, w1, w2, w3, w4,
                list_ref, u0, u1, u2, w_ref, flow_ref, coef, sd, cs,
                wi, wm, wl, wo, b1, b2, b3, b4, t1, t2, cols, h1, h2, h3,
                vx, vy, vz, vys, vzs, xs, xr, ys, yr, zs, zr,
                send_sem, recv_sem, vs_sem, vr_sem, in_sem, out_sem,
                team_send, team_recv, w_in, tally_ref, tally_sem):
    grid = Grid(cx, cy)
    chunks = nf // SUB
    cells = cx * cy
    team = Team()
    listed = list_ref.shape[1]
    def fetch(c, kind, x, n):
        return pltpu.make_async_copy(
            q_hbm.at[pl.ds(c * SUB, SUB), pl.ds(x, n)],
            u0.at[pl.ds(c * SUB, SUB), pl.ds(1 + x, n), pl.ds(SUB, cy)], in_sem.at[c, kind])

    faces = [[fetch(c, 0, 0, 1), fetch(c, 1, cx - 1, 1)] for c in range(chunks)]
    inner = [fetch(c, 2, 1, cx - 2) for c in range(chunks)]
    v_load = pltpu.make_async_copy(
        v_hbm, w_ref.at[:, pl.ds(1, cx), pl.ds(SUB, cy)], in_sem.at[0, 3])
    w_loads = [pltpu.make_async_copy(src, dst, w_in.at[i]) for i, (src, dst) in enumerate((
        (wi_hbm, wi), (b1_hbm, b1), (b2_hbm, b2), (b3_hbm, b3), (b4_hbm, b4),
        (wo_hbm, wo), (list_hbm, list_ref), (wl_hbm, wl), (wm_hbm, wm)))]
    for copy in sum(faces, []) + [v_load] + inner:
        copy.start()
    near = neighbours()
    (xu, xd), (yu, yd), (zu, zd) = near
    halo = Halo(grid, SUB, near, xs, xr, ys, yr, zs, zr, send_sem, recv_sem)
    rows = nf * grid.px * grid.py
    us = [u.reshape(rows, LANES) for u in (u0, u1, u2)]
    vv = w_ref.reshape(3 * grid.px * grid.py, LANES)
    members = [team.member(k) for k in range(team.size)]
    known = [to for pair in near for to in pair] + members[1:]
    greet(known)
    for c in range(chunks):
        for copy in faces[c]:
            copy.wait()
        halo.pack_x(c, us[0], c * SUB)
        if c == 0:
            met(known)
        halo.send_x(c)
    v_load.wait()
    for side, y in ((0, 0), (1, cy - 1)):
        vys[side] = vv[pl.ds(grid.row(1, 0, y), cx, stride=grid.py), :]

    def pack_v(x, _):
        face = jnp.zeros((SUB, LANES), jnp.float32)
        for g in range(grid.groups):
            face = halo.pack_z(face, vv[pl.ds(grid.tile(2, x, g), SUB), :], g)
        vzs[x] = face
        return 0

    lax.fori_loop(0, cx, pack_v, 0)
    plan = [
        (w_ref.at[0, cx, pl.ds(SUB, cy)], vx.at[0], xu),
        (w_ref.at[0, 1, pl.ds(SUB, cy)], vx.at[1], xd),
        (vys.at[1], vy.at[0], yu),
        (vys.at[0], vy.at[1], yd),
        (vzs, vz.at[0], zu),
    ]
    if lax.axis_size("gz") > 2:
        plan.append((vzs, vz.at[1], zd))
    v_copies = [remote(s, d, vs_sem.at[i], vr_sem.at[i], to)
                for i, (s, d, to) in enumerate(plan)]
    for copy in v_copies:
        copy.start()
    for copy in inner:
        copy.wait()
    for copy in w_loads:
        copy.start()
    for c in range(chunks):
        halo.load_z(c, us[0], c * SUB)
        halo.send_yz(c, us[0], c * SUB)

    for copy in w_loads:
        copy.wait()
    count = lax.fori_loop(
        0, listed, lambda i, n: n + jnp.where(list_ref[0, i] >= 0, 1, 0), 0)
    cs[...] = jnp.full((1, LANES), count, jnp.int32)
    cr[0] = cs[...]
    counts = [remote(cs, cr.at[k], team_send.at[chunks, k], team_recv.at[chunks, k], members[k])
              for k in range(1, team.size)]
    for copy in counts:
        copy.start()

    t1[...] = jnp.zeros_like(t1)
    t2[...] = jnp.zeros_like(t2)
    n2, n3 = up(w2.shape[0], LANES), up(w3.shape[0], LANES)
    t1[0:nf, 0:wi.shape[1]] = wi[...].astype(jnp.float32) * 0.5
    bias_rows(t1, nf, 0, b1, 0.5)
    bias_rows(t2, 0, 0, b2, 0.5)
    bias_rows(t2, 0, n2, b3, 0.5)
    bias_rows(t2, 0, n2 + n3, b4, 1.0)
    turned(w1, t1)
    turned(cols, t2)
    widen(w2, wm, 0.5, cols, 0)
    widen(w3, wl, 0.5, cols, n2)
    widen(w4, wo, 1.0, cols, n2 + n3)
    for h in (h1, h2, h3):
        h[h.shape[0] - 16:] = bias_ones(16, LANES).astype(jnp.bfloat16)
    origin = jnp.concatenate(
        [jnp.zeros((nf, LANES), jnp.float32), bias_ones(w1.shape[1] - nf, LANES)], axis=0)
    rest[...] = network(origin.astype(jnp.bfloat16), w1, w2, w3, w4, h1, h2, h3)

    for copy in v_copies:
        copy.wait_recv()
    for side, x in ((0, -1), (1, cx)):
        vv[pl.ds(grid.tile(0, x, 0), cy), :] = vx[side]
    for side, y in ((0, -1), (1, cy)):
        vv[pl.ds(grid.row(1, 0, y), cx, stride=grid.py), :] = vy[side]

    def make_coef(x, _):
        if lax.axis_size("gz") > 2:
            zrow = jnp.where(halo.even, vz[1, x], vz[0, x])
        else:
            zrow = vz[0, x]
        for g in range(grid.groups):
            r0 = grid.tile(0, x, g)
            r1 = grid.tile(1, x, g)
            after, before = halo.z_near(vv[pl.ds(grid.tile(2, x, g), SUB), :], zrow, g)
            values = (
                0.05 - 0.5 * vv[pl.ds(r0 + grid.py, SUB), :],
                0.05 + 0.5 * vv[pl.ds(r0 - grid.py, SUB), :],
                0.05 - 0.5 * vv[pl.ds(r1 + 1, SUB), :],
                0.05 + 0.5 * vv[pl.ds(r1 - 1, SUB), :],
                0.05 - 0.5 * after,
                0.05 + 0.5 * before,
            )
            for i, value in enumerate(values):
                coef[i, x, g] = value
        return 0

    lax.fori_loop(0, cx, make_coef, 0)

    room = flow_ref.shape[1]
    cap = 2 * sd.shape[2]
    flow2 = flow_ref.reshape(nf * room, LANES)
    sends, stores = [], []

    def deal():
        for copy in counts:
            copy.wait_recv()
        tally = pltpu.make_async_copy(cr, tally_ref, tally_sem)
        tally.start()
        tally.wait()
        me = team.place()
        ahead = lax.fori_loop(1, team.size, lambda k, n: n + jnp.where(
            k <= me, tally_ref[k, 0, 0], 0), 0)
        shift = lax.rem(ahead + team.size - me, team.size)
        home = lax.broadcasted_iota(jnp.int32, where_ref.shape, 0) * LANES + (
            lax.broadcasted_iota(jnp.int32, where_ref.shape, 1))
        table = jnp.where(home == cells, shift, team.size * cap)
        for e in range(listed):
            slot = lax.rem(shift + e, team.size) * cap + e // team.size
            table = jnp.where(home == list_ref[0, e], slot, table)
        where_ref[...] = table
        return shift

    def block(c, s, k, shift):
        e = s * team.size + lax.rem(k + team.size - shift, team.size)
        b = jnp.maximum(list_ref[0, jnp.minimum(e, listed - 1)], 0)
        return flow2[pl.ds(c * SUB * room + b, SUB, stride=room), :]

    def dispatch(c, shift):
        for k in range(team.size):
            dst = sd if k else rv
            for p in range(sd.shape[2]):
                pair = [block(c, 2 * p + h, k, shift) for h in range(2)]
                dst[c, k, p] = jnp.concatenate(pair, axis=0).astype(jnp.bfloat16)
        for k in range(1, team.size):
            sends.append(remote(sd.at[c, k], rv.at[c, k], team_send.at[c, k],
                                team_recv.at[c, k], members[k]))
            sends[-1].start()

    for stage in range(3):
        weight = (1.0 / 3.0, 0.5, 1.0)[stage]
        u = us[stage]
        if stage == 1:
            shift = deal()
        for c in range(chunks):
            slot = stage * chunks + c
            first = c * SUB
            halo.receive(slot, u, first)

            def body(i, _):
                for x in [i]:
                    zrow = halo.z_row(slot, x)
                    face = jnp.zeros((SUB, LANES), jnp.float32)
                    for g in range(grid.groups):
                        ks = [coef[j, x, g] for j in range(6)]
                        for f in range(SUB):
                            k = f * grid.groups + g
                            row = grid.tile(first + f, x, g)
                            t = u[pl.ds(row, SUB), :]
                            za, zb = halo.z_near(t, zrow, k)
                            s = (ks[0] * u[pl.ds(row + grid.py, SUB), :]
                                 + ks[1] * u[pl.ds(row - grid.py, SUB), :])
                            s = s + (ks[2] * u[pl.ds(row + 1, SUB), :]
                                     + ks[3] * u[pl.ds(row - 1, SUB), :])
                            s = s + (ks[4] * za + ks[5] * zb)
                            q = t if stage == 0 else us[0][pl.ds(row, SUB), :]
                            r = q + weight * (s - 0.3 * t)
                            if stage == 2:
                                at = pl.multiple_of(x * cy + g * SUB, SUB)
                                flow_ref[first + f, pl.ds(at, SUB)] = r
                            else:
                                us[stage + 1][pl.ds(row, SUB), :] = r
                                face = halo.pack_z(face, r, k)
                    if stage < 2:
                        zs[slot + chunks, x] = face
                return 0

            lax.fori_loop(0, cx, body, 0)
            if stage < 2:
                halo.pack_x(slot + chunks, us[stage + 1], first)
                halo.send_x(slot + chunks)
                halo.send_yz(slot + chunks, us[stage + 1], first)
            else:
                dispatch(c, shift)
                part = pl.ds(first, SUB)
                stores.append(pltpu.make_async_copy(
                    flow_ref.at[part, pl.ds(0, cells)], out_hbm.at[part], out_sem.at[c]))
                stores[-1].start()
    for copy in sends:
        copy.wait_recv()
    for copy in v_copies + counts + sends:
        copy.wait_send()
    for slot in range(3 * chunks):
        halo.finish(slot)
    for copy in stores:
        copy.wait()


def layer(w, src, dst, step):
    rows = dst.shape[0] - 16
    for m in range(0, rows, step):
        k = min(step, rows - m)
        h = jnp.dot(w[m:m + k], src, preferred_element_type=jnp.float32)
        dst[m:m + k] = (h + h * jnp.tanh(h)).astype(jnp.bfloat16)


def network(x, w1, w2, w3, w4, h1, h2, h3):
    layer(w1, x, h1, 400)
    layer(w2, h1[...], h2, 400)
    layer(w3, h2[...], h3, 400)
    return jnp.dot(w4[...], h3[...], preferred_element_type=jnp.float32)


def bias_ones(rows, lanes):
    return jnp.where(lax.broadcasted_iota(jnp.int32, (rows, lanes), 0) < 3, 1.0, 0.0)


def chem_kernel(nf, group, size, count_ref, slots, rest, w1, w2, w3,
                w4, ret_ref, todo, x_in, h1, h2, h3, inc, res):
    n_lanes = group * LANES
    chunks = nf // SUB
    halves = slots.shape[1]
    cap = 2 * halves // size
    x_in[nf:nf + SUB] = bias_ones(SUB, n_lanes)
    for h in (h1, h2, h3):
        h[h.shape[0] - 16:] = bias_ones(16, n_lanes).astype(jnp.bfloat16)
    res[...] = jnp.zeros_like(res)

    me = Team().place()

    def pick(m, carry):
        ahead, n = carry
        k = lax.rem(me + size - m, size)
        have = count_ref[k, 0, 0]
        first = lax.rem(k + 2 * size - lax.rem(ahead + size - m, size), size)
        for s in range(cap):
            todo[n] = k * cap + s
            n = n + jnp.where(s * size + first < have, 1, 0)
        return ahead + have, n

    count = lax.fori_loop(0, size, pick, (0, 0))[1]

    def run(base, blocks):
        part = pl.ds(0, blocks * LANES)
        for i in range(blocks):
            slot = jnp.where(base + i < count, todo[base + i], 0)
            for c in range(chunks):
                tile = slots[c, slot // 2].astype(jnp.float32)
                x_in[c * SUB:(c + 1) * SUB, i * LANES:(i + 1) * LANES] = jnp.where(
                    lax.rem(slot, 2) == 0, tile[:SUB], tile[SUB:])
        inc[:, part] = network(x_in[:, part].astype(jnp.bfloat16), w1, w2, w3, w4,
                               h1.at[:, part], h2.at[:, part], h3.at[:, part])
        for i in range(blocks):
            slot = jnp.where(base + i < count, todo[base + i], size * cap)
            for c in range(chunks):
                res[c, slot] = inc[c * SUB:(c + 1) * SUB, i * LANES:(i + 1) * LANES] - rest[
                    c * SUB:(c + 1) * SUB]

    tail = group // 2
    full = (count + tail - 1) // group
    lax.fori_loop(0, full, lambda g, n: (run(g * group, group), n)[1], 0)

    @pl.when(full * group < count)
    def _():
        run(full * group, tail)

    for c in range(chunks):
        for p in range(halves):
            pair = jnp.concatenate([res[c, 2 * p], res[c, 2 * p + 1]], axis=0)
            ret_ref[c, p] = pair.astype(jnp.bfloat16)


def diffuse_kernel(nf, cx, cy, d_ref, where_ref, owner_ref, q_hbm, ret, rest_ref, out_hbm, act_out,
                   u_ref, old_ref, new_ref, got_ret, res, part, got, act_send, act_recv,
                   xs, xr, ys, yr, zs, zr, send_sem, recv_sem,
                   team_send, team_recv, in_sem, out_sem):
    grid = Grid(cx, cy)
    chunks = nf // SUB
    team = Team()
    pairs = ret.shape[2]
    cells = cx * cy
    cap = 2 * pairs
    loads = []
    for c in range(chunks):
        loads.append(pltpu.make_async_copy(
            q_hbm.at[pl.ds(c * SUB, SUB)],
            old_ref.at[pl.ds(c * SUB, SUB), pl.ds(0, cells)], in_sem.at[c]))
        loads[-1].start()
    near = neighbours()
    groups = [peers(a) for a in AXES[::-1]]
    members = [team.member(team.size - k) for k in range(team.size)]
    known = [to for g in groups for to in g] + members[1:]
    greet(known)
    halo = Halo(grid, SUB, near, xs, xr, ys, yr, zs, zr, send_sem, recv_sem)
    lane = lane_ids()
    u2 = u_ref.reshape(nf * grid.px * grid.py, LANES)
    room = old_ref.shape[1]
    old2 = old_ref.reshape(nf * room, LANES)
    met(known)
    backs = [[remote(ret.at[c, k], got_ret.at[c, k], team_send.at[c, k], team_recv.at[c, k],
                     members[k]) for k in range(1, team.size)] for c in range(chunks)]
    for copies in backs:
        for copy in copies:
            copy.start()

    def hops(phase):
        return [remote(part.at[phase], got.at[phase, k], act_send.at[phase, k],
                       act_recv.at[phase, k], to)
                for k, to in enumerate(groups[phase])]

    def gather(phase):
        for h in hops(phase):
            h.wait_recv()
        total = part[phase]
        for k in range(len(groups[phase])):
            total = total + got[phase, k]
        return total

    flat = lax.broadcasted_iota(jnp.int32, (SUB, LANES), 0) * LANES + lane

    listed = owner_ref.shape[0]

    def heat():
        total = jnp.zeros((SUB, LANES), jnp.float32)
        shift = where_ref[cells // LANES, cells % LANES]

        def body(k, total):
            first = lax.rem(k + team.size - shift, team.size)
            for s in range(cap):
                r = res[0, k * cap + s][0:1]
                warm = jnp.sum(r * r, axis=1, keepdims=True) * (1.0 / (8.0 * LANES))
                e = s * team.size + first
                owner = jnp.where(e < listed, owner_ref[jnp.minimum(e, listed - 1)], -1)
                total = total + jnp.where(flat == owner, warm, 0.0)
            return total

        total = lax.fori_loop(0, team.size, body, total)
        return total

    for c in range(chunks):
        loads[c].wait()
        res[c, team.size * cap] = jnp.zeros((SUB, LANES), jnp.float32)
        rest = rest_ref[c * SUB:(c + 1) * SUB]
        for copy in backs[c]:
            copy.wait_recv()
        for k in range(team.size):
            for p in range(pairs):
                tile = (got_ret if k else ret)[c, k, p].astype(jnp.float32)
                res[c, k * cap + 2 * p] = tile[:SUB] + rest
                res[c, k * cap + 2 * p + 1] = tile[SUB:] + rest

        def add(i, _):
            for x in [i]:
                line, lane0 = x * cy // LANES, lax.rem(x * cy, LANES)
                for y in range(cy):
                    b = x * cy + y
                    if LANES % cy:
                        line, lane0 = b // LANES, lax.rem(b, LANES) - y
                    t = res[c, where_ref[line, lane0 + y]]
                    old = old2[pl.ds(c * SUB * room + b, SUB, stride=room), :]
                    u2[pl.ds(grid.row(c * SUB, x, y), SUB, stride=grid.px * grid.py), :] = old + t
            return 0

        lax.fori_loop(0, cx, add, 0)
        halo.pack_x(c, u2, c * SUB)
        halo.send_x(c)
        halo.load_z(c, u2, c * SUB)
        halo.send_yz(c, u2, c * SUB)
    part[0] = heat()
    for h in hops(0):
        h.start()
    stores = []
    for c in range(chunks):
        if c < len(groups) - 1:
            part[c + 1] = gather(c)
            for h in hops(c + 1):
                h.start()
        first = c * SUB
        halo.receive(c, u2, first)

        def body(i, _):
            for x in [i]:
                zrow = halo.z_row(c, x)
                for f in range(SUB):
                    rate = d_ref[first + f]
                    for g in range(grid.groups):
                        row = grid.tile(first + f, x, g)
                        t = u2[pl.ds(row, SUB), :]
                        za, zb = halo.z_near(t, zrow, f * grid.groups + g)
                        s = u2[pl.ds(row + grid.py, SUB), :] + u2[pl.ds(row - grid.py, SUB), :]
                        s = s + (u2[pl.ds(row + 1, SUB), :] + u2[pl.ds(row - 1, SUB), :])
                        s = s + (za + zb)
                        new_ref[first + f, x, pl.ds(g * SUB, SUB)] = t + rate * (s - 6.0 * t)
            return 0

        lax.fori_loop(0, cx, body, 0)
        chunk = pl.ds(first, SUB)
        stores.append(pltpu.make_async_copy(new_ref.at[chunk], out_hbm.at[chunk], out_sem.at[c]))
        stores[-1].start()
    done = min(chunks, len(groups) - 1)
    for phase in range(done, len(groups) - 1):
        part[phase + 1] = gather(phase)
        for h in hops(phase + 1):
            h.start()
    total = gather(len(groups) - 1)
    me = (lax.axis_index("gx") * lax.axis_size("gy") + lax.axis_index("gy")) * lax.axis_size(
        "gz") + lax.axis_index("gz")
    act_out[0] = jnp.sum(jnp.where(flat == me, total, 0.0))
    for phase in range(len(groups)):
        for h in hops(phase):
            h.wait_send()
    for copies in backs:
        for copy in copies:
            copy.wait_send()
    for c in range(chunks):
        halo.finish(c)
    for copy in stores:
        copy.wait()


def halo_scratch(slots, cx, cy):
    return [
        pltpu.VMEM((slots, 2, SUB, cy, LANES), jnp.bfloat16),
        pltpu.VMEM((slots, 2, SUB, cy, LANES), jnp.bfloat16),
        pltpu.VMEM((slots, 2, SUB, cx, LANES), jnp.float32),
        pltpu.VMEM((slots, 2, SUB, cx, LANES), jnp.float32),
        pltpu.VMEM((slots, cx, SUB, LANES), jnp.float32),
        pltpu.VMEM((slots, 2, cx, SUB, LANES), jnp.float32),
        pltpu.SemaphoreType.DMA((slots, 6)),
        pltpu.SemaphoreType.DMA((slots, 6)),
    ]


def spec(space, n=1):
    return [pl.BlockSpec(memory_space=space)] * n


def local(fields, velocity, diffusivity, weight_in, bias_in, weight_mid, bias_mid,
          weight_low, bias_low, weight_out, bias_out, react_list, owner_table):
    nf, cx, cy, cz = fields.shape
    chunks = nf // SUB
    cells = cx * cy
    box = padded(cx, cy)
    room = odd_tiles(cells)
    slots = 3 * chunks
    dma = pltpu.SemaphoreType.DMA
    f32, bf16 = jnp.float32, jnp.bfloat16
    listed = react_list.shape[1]
    team = Team()
    size, cap = team.size, team.slots(listed)
    traffic = (chunks, size, cap // 2, 2 * SUB, LANES)
    h = (weight_in.shape[1], weight_mid.shape[1], weight_low.shape[1])
    wide = up(h[0], LANES)
    bias_wide = up(h[1], LANES) + up(h[2], LANES) + up(nf, LANES)
    w_shapes = [(wide, 32), (h[1], h[0] + 16), (h[2], h[1] + 16), (nf, h[2] + 16)]

    flowed, sent, counts, where, rest, w1, w2, w3, w4 = pl.pallas_call(
        functools.partial(flow_kernel, nf, cx, cy),
        out_shape=(jax.ShapeDtypeStruct((nf, cells, cz), f32),
                   jax.ShapeDtypeStruct(traffic, bf16),
                   jax.ShapeDtypeStruct((size, 1, LANES), jnp.int32),
                   jax.ShapeDtypeStruct((up(cells + 1, SUB * LANES) // LANES, LANES), jnp.int32),
                   jax.ShapeDtypeStruct((nf, LANES), f32))
        + tuple(jax.ShapeDtypeStruct(w, bf16) for w in w_shapes),
        in_specs=spec(pltpu.HBM, 11),
        out_specs=tuple(spec(pl.ANY) + spec(pltpu.VMEM, 8)),
        scratch_shapes=[pltpu.SMEM((1, listed), jnp.int32)]
        + [pltpu.VMEM((nf,) + box, f32)] * 3 + [
            pltpu.VMEM((3,) + box, f32),
            pltpu.VMEM((nf, room, cz), f32),
            pltpu.VMEM((6, cx, cy // SUB, SUB, cz), f32),
            pltpu.VMEM(traffic, bf16),
            pltpu.VMEM((1, LANES), jnp.int32),
            pltpu.VMEM((nf, h[0]), bf16),
            pltpu.VMEM((h[1], h[0]), bf16),
            pltpu.VMEM((h[2], h[1]), bf16),
            pltpu.VMEM((nf, h[2]), bf16),
            pltpu.VMEM((h[0],), f32),
            pltpu.VMEM((h[1],), f32),
            pltpu.VMEM((h[2],), f32),
            pltpu.VMEM((nf,), f32),
            pltpu.VMEM((32, wide), f32),
            pltpu.VMEM((32, bias_wide), f32),
            pltpu.VMEM((bias_wide, 32), bf16),
            pltpu.VMEM((h[0] + 16, LANES), bf16),
            pltpu.VMEM((h[1] + 16, LANES), bf16),
            pltpu.VMEM((h[2] + 16, LANES), bf16),
            pltpu.VMEM((2, cy, cz), f32),
            pltpu.VMEM((2, cx, cz), f32),
            pltpu.VMEM((2, cx, SUB, cz), f32),
            pltpu.VMEM((2, cx, cz), f32),
            pltpu.VMEM((cx, SUB, cz), f32),
        ] + halo_scratch(slots, cx, cy) + [
            dma((6,)), dma((6,)), dma((chunks, 4)), dma((chunks,)),
            dma((chunks + 1, size)), dma((chunks + 1, size)), dma((9,)),
            pltpu.SMEM((size, 1, LANES), jnp.int32), dma],
        compiler_params=pltpu.CompilerParams(
            collective_id=0, has_side_effects=True, vmem_limit_bytes=48 * MIB),
        name="flow",
    )(*[pltpu.with_memory_space_constraint(a, pltpu.HBM) for a in (
        react_list, fields, velocity, weight_in, weight_mid.T, weight_low.T, weight_out.T,
        bias_in, bias_mid, bias_low, bias_out)])

    group = 8
    n_lanes = group * LANES
    halves = size * cap // 2
    ret = pl.pallas_call(
        functools.partial(chem_kernel, nf, group, size),
        out_shape=jax.ShapeDtypeStruct((chunks, halves, 2 * SUB, LANES), bf16),
        in_specs=spec(pltpu.SMEM) + spec(pltpu.VMEM, 6),
        out_specs=spec(pltpu.VMEM)[0],
        scratch_shapes=[
            pltpu.SMEM((size * cap + 2 * group,), jnp.int32),
            pltpu.VMEM((nf + SUB, n_lanes), f32),
            pltpu.VMEM((h[0] + 16, n_lanes), bf16),
            pltpu.VMEM((h[1] + 16, n_lanes), bf16),
            pltpu.VMEM((h[2] + 16, n_lanes), bf16),
            pltpu.VMEM((nf, n_lanes), f32),
            pltpu.VMEM((chunks, size * cap + 1, SUB, LANES), f32),
        ],
        compiler_params=pltpu.CompilerParams(vmem_limit_bytes=40 * MIB),
        name="chem",
    )(counts, sent.reshape(chunks, halves, 2 * SUB, LANES), rest,
      w1, w2, w3, w4)

    most = max(lax.axis_size(a) for a in AXES) - 1
    updated, mine = pl.pallas_call(
        functools.partial(diffuse_kernel, nf, cx, cy),
        out_shape=(jax.ShapeDtypeStruct(fields.shape, f32),
                   jax.ShapeDtypeStruct((1,), f32)),
        in_specs=spec(pltpu.SMEM, 3) + spec(pl.ANY) + spec(pltpu.VMEM, 2),
        out_specs=(spec(pl.ANY)[0], spec(pltpu.SMEM)[0]),
        scratch_shapes=[
            pltpu.VMEM((nf,) + box, f32),
            pltpu.VMEM((nf, room, cz), f32),
            pltpu.VMEM((nf, cx, cy, cz), f32),
            pltpu.VMEM(traffic, bf16),
            pltpu.VMEM((chunks, size * cap + 1, SUB, LANES), f32),
            pltpu.VMEM((len(AXES), SUB, LANES), f32),
            pltpu.VMEM((len(AXES), most, SUB, LANES), f32),
            dma((len(AXES), most)),
            dma((len(AXES), most)),
        ] + halo_scratch(chunks, cx, cy) + [
            dma((chunks, size)), dma((chunks, size)), dma((chunks,)), dma((chunks,))],
        compiler_params=pltpu.CompilerParams(
            collective_id=1, has_side_effects=True, vmem_limit_bytes=48 * MIB),
        name="diffuse",
    )(diffusivity, where, owner_table[0], flowed, ret.reshape(traffic), rest)
    return updated, mine


def solution(mesh):
    return jax.shard_map(
        local,
        mesh=mesh,
        in_specs=(P(None, *AXES), P(None, *AXES)) + (P(),) * 9
        + (P(AXES, None), P(AXES, None)),
        out_specs=(P(None, *AXES), P(AXES)),
        check_vma=False,
    )
```

```python
import functools

import jax
import jax.numpy as jnp
from jax import lax
from jax.experimental import pallas as pl
from jax.experimental.pallas import tpu as pltpu
from jax.sharding import PartitionSpec as P

AXES = ("gx", "gy", "gz")
MESH = pl.DeviceIdType.MESH
SUB = 8
LANES = 128
MIB = 1024 * 1024


def neighbours():
    ids = {a: lax.axis_index(a) for a in AXES}
    out = []
    for a in AXES:
        n = lax.axis_size(a)
        up = dict(ids)
        up[a] = lax.rem(ids[a] + 1, n)
        down = dict(ids)
        down[a] = lax.rem(ids[a] + n - 1, n)
        out.append((tuple(up[b] for b in AXES), tuple(down[b] for b in AXES)))
    return out


def greet(targets):
    barrier = pltpu.get_barrier_semaphore()
    for to in targets:
        pl.semaphore_signal(barrier, inc=1, device_id=to, device_id_type=MESH)


def met(targets):
    pl.semaphore_wait(pltpu.get_barrier_semaphore(), len(targets))


def peers(axis):
    ids = {a: lax.axis_index(a) for a in AXES}
    n = lax.axis_size(axis)
    out = []
    for k in range(1, n):
        to = dict(ids)
        to[axis] = lax.rem(ids[axis] + k, n)
        out.append(tuple(to[b] for b in AXES))
    return out


def remote(src, dst, send, recv, to):
    return pltpu.make_async_remote_copy(
        src_ref=src, dst_ref=dst, send_sem=send, recv_sem=recv,
        device_id=to, device_id_type=MESH)


def lane_ids():
    return lax.broadcasted_iota(jnp.int32, (SUB, LANES), 1)


def odd_tiles(n):
    return n if n // SUB % 2 else n + SUB


def padded(cx, cy):
    return cx + 2 + (cx + 1) % 2, odd_tiles(cy + 2 * SUB), LANES


class Grid:
    def __init__(self, cx, cy):
        self.cx, self.cy = cx, cy
        self.px, self.py, _ = padded(cx, cy)
        self.groups = cy // SUB

    def row(self, f, x, y=0):
        return (f * self.px + x + 1) * self.py + SUB + y

    def tile(self, f, x, g):
        r = (f * self.px + x + 1) * self.py + SUB + g * SUB
        return r if isinstance(r, int) else pl.multiple_of(r, SUB)


class Halo:
    def __init__(self, grid, width, near, xs, xr, ys, yr, zs, zr, send_sem, recv_sem):
        self.grid, self.width, self.near = grid, width, near
        self.xs, self.xr, self.ys, self.yr = xs, xr, ys, yr
        self.zs, self.zr, self.send_sem, self.recv_sem = zs, zr, send_sem, recv_sem
        lane = lane_ids()
        self.first, self.last = lane == 0, lane == LANES - 1
        self.even = lax.rem(lane, 2) == 0
        self.pair = lax.rem(lane + 1, LANES) // 2

    def copies(self, slot, first=0, last=6):
        (xu, xd), (yu, yd), (zu, zd) = self.near
        plan = [
            (self.xs.at[slot, 1], self.xr.at[slot, 0], xu),
            (self.xs.at[slot, 0], self.xr.at[slot, 1], xd),
            (self.ys.at[slot, 1], self.yr.at[slot, 0], yu),
            (self.ys.at[slot, 0], self.yr.at[slot, 1], yd),
            (self.zs.at[slot], self.zr.at[slot, 0], zu),
        ]
        if lax.axis_size("gz") > 2:
            plan.append((self.zs.at[slot], self.zr.at[slot, 1], zd))
        return [
            remote(s, d, self.send_sem.at[slot, i], self.recv_sem.at[slot, i], to)
            for i, (s, d, to) in enumerate(plan) if first <= i < last
        ]

    def pack_z(self, face, t, k):
        return jnp.where(self.pair == k, pltpu.roll(t, 2 * k, 1) if k else t, face)

    def z_row(self, slot, x):
        if lax.axis_size("gz") > 2:
            return jnp.where(self.even, self.zr[slot, 1, x], self.zr[slot, 0, x])
        return self.zr[slot, 0, x]

    def z_near(self, t, zrow, k):
        r = pltpu.roll(zrow, LANES - 2 * k, 1) if k else zrow
        after = pltpu.roll(jnp.where(self.first, r, t), LANES - 1, 1)
        before = pltpu.roll(jnp.where(self.last, r, t), 1, 1)
        return after, before

    def pack_x(self, slot, u, base):
        grid = self.grid
        for f in range(self.width):
            for side, x in ((0, 0), (1, grid.cx - 1)):
                self.xs[slot, side, f] = u[
                    pl.ds(grid.tile(base + f, x, 0), grid.cy), :].astype(jnp.bfloat16)

    def send_x(self, slot):
        for c in self.copies(slot, 0, 2):
            c.start()

    def send_yz(self, slot, u, base):
        grid = self.grid
        for f in range(self.width):
            for side, y in ((0, 0), (1, grid.cy - 1)):
                self.ys[slot, side, f] = u[
                    pl.ds(grid.row(base + f, 0, y), grid.cx, stride=grid.py), :]
        for c in self.copies(slot, 2):
            c.start()

    def load_z(self, slot, u, base):
        grid = self.grid

        def body(i, _):
            for x in [i]:
                face = jnp.zeros((SUB, LANES), jnp.float32)
                for g in range(grid.groups):
                    for f in range(self.width):
                        t = u[pl.ds(grid.tile(base + f, x, g), SUB), :]
                        face = self.pack_z(face, t, f * grid.groups + g)
                self.zs[slot, x] = face
            return 0

        lax.fori_loop(0, grid.cx, body, 0)

    def receive(self, slot, u, base):
        grid = self.grid
        for c in self.copies(slot):
            c.wait_recv()
        for f in range(self.width):
            for side, x in ((0, -1), (1, grid.cx)):
                u[pl.ds(grid.tile(base + f, x, 0), grid.cy), :] = self.xr[
                    slot, side, f].astype(jnp.float32)
            for side, y in ((0, -1), (1, grid.cy)):
                u[pl.ds(grid.row(base + f, 0, y), grid.cx, stride=grid.py), :] = self.yr[
                    slot, side, f]

    def finish(self, slot):
        for c in self.copies(slot):
            c.wait_send()


class Team:
    def __init__(self):
        self.nx, self.ny, self.nz = (lax.axis_size(a) for a in AXES)
        self.span = 2 if self.ny % 2 == 0 else self.ny
        self.size = self.nx * self.span * self.nz

    def slots(self, listed):
        return 2 * ((listed + 2 * self.size - 1) // (2 * self.size))

    def place(self):
        i, j, k = (lax.axis_index(a) for a in AXES)
        return (i * self.span + lax.rem(j, self.span)) * self.nz + k

    def member(self, step):
        m = lax.rem(self.place() + step, self.size)
        i = m // (self.span * self.nz)
        j = lax.rem(m // self.nz, self.span)
        j = j + (lax.axis_index("gy") // self.span) * self.span
        return (i, j, lax.rem(m, self.nz))


def bias_rows(dst, row, lane, bias, scale):
    n = bias.shape[0]
    rest = bias[...].reshape(1, n) * scale
    for i in range(3):
        part = rest.astype(jnp.bfloat16).astype(jnp.float32)
        rest = rest - part
        dst[row + i:row + i + 1, lane:lane + n] = part


def turned(dst, src):
    for j in range(0, src.shape[1], LANES):
        dst[j:j + LANES] = src[:, j:j + LANES].T.astype(jnp.bfloat16)


def widen(dst, src, scale, cols, first):
    rows, k = src.shape
    step = 16 if rows % 16 == 0 else rows

    def body(j, _):
        at = pl.ds(pl.multiple_of(j * step, step), step)
        dst[at, pl.ds(0, k)] = src[at, :] * jnp.bfloat16(scale)
        dst[at, pl.ds(k, 16)] = cols[pl.ds(pl.multiple_of(first + j * step, 8), step),
                                     pl.ds(0, 16)]
        return 0

    lax.fori_loop(0, rows // step, body, 0)


def up(n, m):
    return (n + m - 1) // m * m


def flow_kernel(nf, cx, cy, list_hbm, q_hbm, v_hbm, wi_hbm, wm_hbm, wl_hbm, wo_hbm,
                b1_hbm, b2_hbm, b3_hbm, b4_hbm,
                out_hbm, rv, cr, where_ref, rest, w1, w2, w3, w4,
                list_ref, u0, u1, u2, w_ref, flow_ref, coef, sd, cs,
                wi, wm, wl, wo, b1, b2, b3, b4, t1, t2, cols, h1, h2, h3,
                vx, vy, vz, vys, vzs, xs, xr, ys, yr, zs, zr,
                send_sem, recv_sem, vs_sem, vr_sem, in_sem, out_sem,
                team_send, team_recv, w_in, tally_ref, tally_sem):
    grid = Grid(cx, cy)
    chunks = nf // SUB
    cells = cx * cy
    team = Team()
    listed = list_ref.shape[1]
    def fetch(c, kind, x, n):
        return pltpu.make_async_copy(
            q_hbm.at[pl.ds(c * SUB, SUB), pl.ds(x, n)],
            u0.at[pl.ds(c * SUB, SUB), pl.ds(1 + x, n), pl.ds(SUB, cy)], in_sem.at[c, kind])

    faces = [[fetch(c, 0, 0, 1), fetch(c, 1, cx - 1, 1)] for c in range(chunks)]
    inner = [fetch(c, 2, 1, cx - 2) for c in range(chunks)]
    v_load = pltpu.make_async_copy(
        v_hbm, w_ref.at[:, pl.ds(1, cx), pl.ds(SUB, cy)], in_sem.at[0, 3])
    w_loads = [pltpu.make_async_copy(src, dst, w_in.at[i]) for i, (src, dst) in enumerate((
        (wi_hbm, wi), (b1_hbm, b1), (b2_hbm, b2), (b3_hbm, b3), (b4_hbm, b4),
        (wo_hbm, wo), (list_hbm, list_ref), (wl_hbm, wl), (wm_hbm, wm)))]
    for copy in sum(faces, []) + [v_load] + inner + w_loads:
        copy.start()
    near = neighbours()
    (xu, xd), (yu, yd), (zu, zd) = near
    halo = Halo(grid, SUB, near, xs, xr, ys, yr, zs, zr, send_sem, recv_sem)
    rows = nf * grid.px * grid.py
    us = [u.reshape(rows, LANES) for u in (u0, u1, u2)]
    vv = w_ref.reshape(3 * grid.px * grid.py, LANES)
    members = [team.member(k) for k in range(team.size)]
    known = [to for pair in near for to in pair] + members[1:]
    greet(known)
    for c in range(chunks):
        for copy in faces[c]:
            copy.wait()
        halo.pack_x(c, us[0], c * SUB)
        if c == 0:
            met(known)
        halo.send_x(c)
    v_load.wait()
    for side, y in ((0, 0), (1, cy - 1)):
        vys[side] = vv[pl.ds(grid.row(1, 0, y), cx, stride=grid.py), :]

    def pack_v(x, _):
        face = jnp.zeros((SUB, LANES), jnp.float32)
        for g in range(grid.groups):
            face = halo.pack_z(face, vv[pl.ds(grid.tile(2, x, g), SUB), :], g)
        vzs[x] = face
        return 0

    lax.fori_loop(0, cx, pack_v, 0)
    plan = [
        (w_ref.at[0, cx, pl.ds(SUB, cy)], vx.at[0], xu),
        (w_ref.at[0, 1, pl.ds(SUB, cy)], vx.at[1], xd),
        (vys.at[1], vy.at[0], yu),
        (vys.at[0], vy.at[1], yd),
        (vzs, vz.at[0], zu),
    ]
    if lax.axis_size("gz") > 2:
        plan.append((vzs, vz.at[1], zd))
    v_copies = [remote(s, d, vs_sem.at[i], vr_sem.at[i], to)
                for i, (s, d, to) in enumerate(plan)]
    for copy in v_copies:
        copy.start()
    for copy in inner:
        copy.wait()
    for c in range(chunks):
        halo.load_z(c, us[0], c * SUB)
        halo.send_yz(c, us[0], c * SUB)

    for copy in w_loads:
        copy.wait()
    count = lax.fori_loop(
        0, listed, lambda i, n: n + jnp.where(list_ref[0, i] >= 0, 1, 0), 0)
    cs[...] = jnp.full((1, LANES), count, jnp.int32)
    cr[0] = cs[...]
    counts = [remote(cs, cr.at[k], team_send.at[chunks, k], team_recv.at[chunks, k], members[k])
              for k in range(1, team.size)]
    for copy in counts:
        copy.start()

    t1[...] = jnp.zeros_like(t1)
    t2[...] = jnp.zeros_like(t2)
    n2, n3 = up(w2.shape[0], LANES), up(w3.shape[0], LANES)
    t1[0:nf, 0:wi.shape[1]] = wi[...].astype(jnp.float32) * 0.5
    bias_rows(t1, nf, 0, b1, 0.5)
    bias_rows(t2, 0, 0, b2, 0.5)
    bias_rows(t2, 0, n2, b3, 0.5)
    bias_rows(t2, 0, n2 + n3, b4, 1.0)
    turned(w1, t1)
    turned(cols, t2)
    widen(w2, wm, 0.5, cols, 0)
    widen(w3, wl, 0.5, cols, n2)
    widen(w4, wo, 1.0, cols, n2 + n3)

    for copy in v_copies:
        copy.wait_recv()
    for side, x in ((0, -1), (1, cx)):
        vv[pl.ds(grid.tile(0, x, 0), cy), :] = vx[side]
    for side, y in ((0, -1), (1, cy)):
        vv[pl.ds(grid.row(1, 0, y), cx, stride=grid.py), :] = vy[side]

    def make_coef(x, _):
        if lax.axis_size("gz") > 2:
            zrow = jnp.where(halo.even, vz[1, x], vz[0, x])
        else:
            zrow = vz[0, x]
        for g in range(grid.groups):
            r0 = grid.tile(0, x, g)
            r1 = grid.tile(1, x, g)
            after, before = halo.z_near(vv[pl.ds(grid.tile(2, x, g), SUB), :], zrow, g)
            values = (
                0.05 - 0.5 * vv[pl.ds(r0 + grid.py, SUB), :],
                0.05 + 0.5 * vv[pl.ds(r0 - grid.py, SUB), :],
                0.05 - 0.5 * vv[pl.ds(r1 + 1, SUB), :],
                0.05 + 0.5 * vv[pl.ds(r1 - 1, SUB), :],
                0.05 - 0.5 * after,
                0.05 + 0.5 * before,
            )
            for i, value in enumerate(values):
                coef[i, x, g] = value
        return 0

    lax.fori_loop(0, cx, make_coef, 0)

    room = flow_ref.shape[1]
    cap = 2 * sd.shape[2]
    flow2 = flow_ref.reshape(nf * room, LANES)
    sends, stores = [], []

    def settle():
        for h in (h1, h2, h3):
            h[h.shape[0] - 16:] = bias_ones(16, LANES).astype(jnp.bfloat16)
        origin = jnp.concatenate(
            [jnp.zeros((nf, LANES), jnp.float32), bias_ones(w1.shape[1] - nf, LANES)], axis=0)
        rest[...] = network(origin.astype(jnp.bfloat16), w1, w2, w3, w4, h1, h2, h3)

    def deal():
        for copy in counts:
            copy.wait_recv()
        tally = pltpu.make_async_copy(cr, tally_ref, tally_sem)
        tally.start()
        tally.wait()
        me = team.place()
        ahead = lax.fori_loop(1, team.size, lambda k, n: n + jnp.where(
            k <= me, tally_ref[k, 0, 0], 0), 0)
        shift = lax.rem(ahead + team.size - me, team.size)
        home = lax.broadcasted_iota(jnp.int32, where_ref.shape, 0) * LANES + (
            lax.broadcasted_iota(jnp.int32, where_ref.shape, 1))
        table = jnp.where(home == cells, shift, team.size * cap)
        for e in range(listed):
            slot = lax.rem(shift + e, team.size) * cap + e // team.size
            table = jnp.where(home == list_ref[0, e], slot, table)
        where_ref[...] = table
        return shift

    def block(c, s, k, shift):
        e = s * team.size + lax.rem(k + team.size - shift, team.size)
        b = jnp.maximum(list_ref[0, jnp.minimum(e, listed - 1)], 0)
        return flow2[pl.ds(c * SUB * room + b, SUB, stride=room), :]

    def dispatch(c, shift):
        for k in range(team.size):
            dst = sd if k else rv
            for p in range(sd.shape[2]):
                pair = [block(c, 2 * p + h, k, shift) for h in range(2)]
                dst[c, k, p] = jnp.concatenate(pair, axis=0).astype(jnp.bfloat16)
        for k in range(1, team.size):
            sends.append(remote(sd.at[c, k], rv.at[c, k], team_send.at[c, k],
                                team_recv.at[c, k], members[k]))
            sends[-1].start()

    for stage in range(3):
        weight = (1.0 / 3.0, 0.5, 1.0)[stage]
        u = us[stage]
        if stage == 1:
            shift = deal()
        if stage == 2:
            settle()
        for c in range(chunks):
            slot = stage * chunks + c
            first = c * SUB
            halo.receive(slot, u, first)

            def body(i, _):
                for x in [i]:
                    zrow = halo.z_row(slot, x)
                    face = jnp.zeros((SUB, LANES), jnp.float32)
                    for g in range(grid.groups):
                        ks = [coef[j, x, g] for j in range(6)]
                        for f in range(SUB):
                            k = f * grid.groups + g
                            row = grid.tile(first + f, x, g)
                            t = u[pl.ds(row, SUB), :]
                            za, zb = halo.z_near(t, zrow, k)
                            s = (ks[0] * u[pl.ds(row + grid.py, SUB), :]
                                 + ks[1] * u[pl.ds(row - grid.py, SUB), :])
                            s = s + (ks[2] * u[pl.ds(row + 1, SUB), :]
                                     + ks[3] * u[pl.ds(row - 1, SUB), :])
                            s = s + (ks[4] * za + ks[5] * zb)
                            q = t if stage == 0 else us[0][pl.ds(row, SUB), :]
                            r = q + weight * (s - 0.3 * t)
                            if stage == 2:
                                at = pl.multiple_of(x * cy + g * SUB, SUB)
                                flow_ref[first + f, pl.ds(at, SUB)] = r
                            else:
                                us[stage + 1][pl.ds(row, SUB), :] = r
                                face = halo.pack_z(face, r, k)
                    if stage < 2:
                        zs[slot + chunks, x] = face
                return 0

            lax.fori_loop(0, cx, body, 0)
            if stage < 2:
                halo.pack_x(slot + chunks, us[stage + 1], first)
                halo.send_x(slot + chunks)
                halo.send_yz(slot + chunks, us[stage + 1], first)
            else:
                dispatch(c, shift)
                part = pl.ds(first, SUB)
                stores.append(pltpu.make_async_copy(
                    flow_ref.at[part, pl.ds(0, cells)], out_hbm.at[part], out_sem.at[c]))
                stores[-1].start()
    for copy in sends:
        copy.wait_recv()
    for copy in v_copies + counts + sends:
        copy.wait_send()
    for slot in range(3 * chunks):
        halo.finish(slot)
    for copy in stores:
        copy.wait()


def layer(w, src, dst, step):
    rows = dst.shape[0] - 16
    for m in range(0, rows, step):
        k = min(step, rows - m)
        h = jnp.dot(w[m:m + k], src, preferred_element_type=jnp.float32)
        dst[m:m + k] = (h + h * jnp.tanh(h)).astype(jnp.bfloat16)


def network(x, w1, w2, w3, w4, h1, h2, h3):
    layer(w1, x, h1, 400)
    layer(w2, h1[...], h2, 400)
    layer(w3, h2[...], h3, 400)
    return jnp.dot(w4[...], h3[...], preferred_element_type=jnp.float32)


def bias_ones(rows, lanes):
    return jnp.where(lax.broadcasted_iota(jnp.int32, (rows, lanes), 0) < 3, 1.0, 0.0)


def chem_kernel(nf, group, size, count_ref, slots, rest, w1, w2, w3,
                w4, ret_ref, todo, x_in, h1, h2, h3, inc, res):
    n_lanes = group * LANES
    chunks = nf // SUB
    halves = slots.shape[1]
    cap = 2 * halves // size
    x_in[nf:nf + SUB] = bias_ones(SUB, n_lanes)
    for h in (h1, h2, h3):
        h[h.shape[0] - 16:] = bias_ones(16, n_lanes).astype(jnp.bfloat16)
    res[...] = jnp.zeros_like(res)

    me = Team().place()

    def pick(m, carry):
        ahead, n = carry
        k = lax.rem(me + size - m, size)
        have = count_ref[k, 0, 0]
        first = lax.rem(k + 2 * size - lax.rem(ahead + size - m, size), size)
        for s in range(cap):
            todo[n] = k * cap + s
            n = n + jnp.where(s * size + first < have, 1, 0)
        return ahead + have, n

    count = lax.fori_loop(0, size, pick, (0, 0))[1]

    def run(base, blocks):
        part = pl.ds(0, blocks * LANES)
        for i in range(blocks):
            slot = jnp.where(base + i < count, todo[base + i], 0)
            for c in range(chunks):
                tile = slots[c, slot // 2].astype(jnp.float32)
                x_in[c * SUB:(c + 1) * SUB, i * LANES:(i + 1) * LANES] = jnp.where(
                    lax.rem(slot, 2) == 0, tile[:SUB], tile[SUB:])
        inc[:, part] = network(x_in[:, part].astype(jnp.bfloat16), w1, w2, w3, w4,
                               h1.at[:, part], h2.at[:, part], h3.at[:, part])
        for i in range(blocks):
            slot = jnp.where(base + i < count, todo[base + i], size * cap)
            for c in range(chunks):
                res[c, slot] = inc[c * SUB:(c + 1) * SUB, i * LANES:(i + 1) * LANES] - rest[
                    c * SUB:(c + 1) * SUB]

    tail = group // 2
    full = (count + tail - 1) // group
    lax.fori_loop(0, full, lambda g, n: (run(g * group, group), n)[1], 0)

    @pl.when(full * group < count)
    def _():
        run(full * group, tail)

    for c in range(chunks):
        for p in range(halves):
            pair = jnp.concatenate([res[c, 2 * p], res[c, 2 * p + 1]], axis=0)
            ret_ref[c, p] = pair.astype(jnp.bfloat16)


def diffuse_kernel(nf, cx, cy, d_ref, where_ref, owner_ref, q_hbm, ret, rest_ref, out_hbm, act_out,
                   u_ref, old_ref, new_ref, got_ret, res, part, got, act_send, act_recv,
                   xs, xr, ys, yr, zs, zr, send_sem, recv_sem,
                   team_send, team_recv, in_sem, out_sem):
    grid = Grid(cx, cy)
    chunks = nf // SUB
    team = Team()
    pairs = ret.shape[2]
    cells = cx * cy
    cap = 2 * pairs
    loads = []
    for c in range(chunks):
        loads.append(pltpu.make_async_copy(
            q_hbm.at[pl.ds(c * SUB, SUB)],
            old_ref.at[pl.ds(c * SUB, SUB), pl.ds(0, cells)], in_sem.at[c]))
        loads[-1].start()
    near = neighbours()
    groups = [peers(a) for a in AXES[::-1]]
    members = [team.member(team.size - k) for k in range(team.size)]
    known = [to for g in groups for to in g] + members[1:]
    greet(known)
    halo = Halo(grid, SUB, near, xs, xr, ys, yr, zs, zr, send_sem, recv_sem)
    lane = lane_ids()
    u2 = u_ref.reshape(nf * grid.px * grid.py, LANES)
    room = old_ref.shape[1]
    old2 = old_ref.reshape(nf * room, LANES)
    met(known)
    backs = [[remote(ret.at[c, k], got_ret.at[c, k], team_send.at[c, k], team_recv.at[c, k],
                     members[k]) for k in range(1, team.size)] for c in range(chunks)]
    for copies in backs:
        for copy in copies:
            copy.start()

    def hops(phase):
        return [remote(part.at[phase], got.at[phase, k], act_send.at[phase, k],
                       act_recv.at[phase, k], to)
                for k, to in enumerate(groups[phase])]

    def gather(phase):
        for h in hops(phase):
            h.wait_recv()
        total = part[phase]
        for k in range(len(groups[phase])):
            total = total + got[phase, k]
        return total

    flat = lax.broadcasted_iota(jnp.int32, (SUB, LANES), 0) * LANES + lane

    listed = owner_ref.shape[0]

    def heat():
        total = jnp.zeros((SUB, LANES), jnp.float32)
        shift = where_ref[cells // LANES, cells % LANES]

        def body(k, total):
            first = lax.rem(k + team.size - shift, team.size)
            for s in range(cap):
                r = res[0, k * cap + s][0:1]
                warm = jnp.sum(r * r, axis=1, keepdims=True) * (1.0 / (8.0 * LANES))
                e = s * team.size + first
                owner = jnp.where(e < listed, owner_ref[jnp.minimum(e, listed - 1)], -1)
                total = total + jnp.where(flat == owner, warm, 0.0)
            return total

        total = lax.fori_loop(0, team.size, body, total)
        return total

    for c in range(chunks):
        loads[c].wait()
        res[c, team.size * cap] = jnp.zeros((SUB, LANES), jnp.float32)
        rest = rest_ref[c * SUB:(c + 1) * SUB]
        for copy in backs[c]:
            copy.wait_recv()
        for k in range(team.size):
            for p in range(pairs):
                tile = (got_ret if k else ret)[c, k, p].astype(jnp.float32)
                res[c, k * cap + 2 * p] = tile[:SUB] + rest
                res[c, k * cap + 2 * p + 1] = tile[SUB:] + rest

        def add(i, _):
            for x in [i]:
                line, lane0 = x * cy // LANES, lax.rem(x * cy, LANES)
                for y in range(cy):
                    b = x * cy + y
                    if LANES % cy:
                        line, lane0 = b // LANES, lax.rem(b, LANES) - y
                    t = res[c, where_ref[line, lane0 + y]]
                    old = old2[pl.ds(c * SUB * room + b, SUB, stride=room), :]
                    u2[pl.ds(grid.row(c * SUB, x, y), SUB, stride=grid.px * grid.py), :] = old + t
            return 0

        lax.fori_loop(0, cx, add, 0)
        halo.pack_x(c, u2, c * SUB)
        halo.send_x(c)
        halo.load_z(c, u2, c * SUB)
        halo.send_yz(c, u2, c * SUB)
    part[0] = heat()
    for h in hops(0):
        h.start()
    stores = []
    for c in range(chunks):
        if c < len(groups) - 1:
            part[c + 1] = gather(c)
            for h in hops(c + 1):
                h.start()
        first = c * SUB
        halo.receive(c, u2, first)

        def body(i, _):
            for x in [i]:
                zrow = halo.z_row(c, x)
                for f in range(SUB):
                    rate = d_ref[first + f]
                    for g in range(grid.groups):
                        row = grid.tile(first + f, x, g)
                        t = u2[pl.ds(row, SUB), :]
                        za, zb = halo.z_near(t, zrow, f * grid.groups + g)
                        s = u2[pl.ds(row + grid.py, SUB), :] + u2[pl.ds(row - grid.py, SUB), :]
                        s = s + (u2[pl.ds(row + 1, SUB), :] + u2[pl.ds(row - 1, SUB), :])
                        s = s + (za + zb)
                        new_ref[first + f, x, pl.ds(g * SUB, SUB)] = t + rate * (s - 6.0 * t)
            return 0

        lax.fori_loop(0, cx, body, 0)
        chunk = pl.ds(first, SUB)
        stores.append(pltpu.make_async_copy(new_ref.at[chunk], out_hbm.at[chunk], out_sem.at[c]))
        stores[-1].start()
    done = min(chunks, len(groups) - 1)
    for phase in range(done, len(groups) - 1):
        part[phase + 1] = gather(phase)
        for h in hops(phase + 1):
            h.start()
    total = gather(len(groups) - 1)
    me = (lax.axis_index("gx") * lax.axis_size("gy") + lax.axis_index("gy")) * lax.axis_size(
        "gz") + lax.axis_index("gz")
    act_out[0] = jnp.sum(jnp.where(flat == me, total, 0.0))
    for phase in range(len(groups)):
        for h in hops(phase):
            h.wait_send()
    for copies in backs:
        for copy in copies:
            copy.wait_send()
    for c in range(chunks):
        halo.finish(c)
    for copy in stores:
        copy.wait()


def halo_scratch(slots, cx, cy):
    return [
        pltpu.VMEM((slots, 2, SUB, cy, LANES), jnp.bfloat16),
        pltpu.VMEM((slots, 2, SUB, cy, LANES), jnp.bfloat16),
        pltpu.VMEM((slots, 2, SUB, cx, LANES), jnp.float32),
        pltpu.VMEM((slots, 2, SUB, cx, LANES), jnp.float32),
        pltpu.VMEM((slots, cx, SUB, LANES), jnp.float32),
        pltpu.VMEM((slots, 2, cx, SUB, LANES), jnp.float32),
        pltpu.SemaphoreType.DMA((slots, 6)),
        pltpu.SemaphoreType.DMA((slots, 6)),
    ]


def spec(space, n=1):
    return [pl.BlockSpec(memory_space=space)] * n


def local(fields, velocity, diffusivity, weight_in, bias_in, weight_mid, bias_mid,
          weight_low, bias_low, weight_out, bias_out, react_list, owner_table):
    nf, cx, cy, cz = fields.shape
    chunks = nf // SUB
    cells = cx * cy
    box = padded(cx, cy)
    room = odd_tiles(cells)
    slots = 3 * chunks
    dma = pltpu.SemaphoreType.DMA
    f32, bf16 = jnp.float32, jnp.bfloat16
    listed = react_list.shape[1]
    team = Team()
    size, cap = team.size, team.slots(listed)
    traffic = (chunks, size, cap // 2, 2 * SUB, LANES)
    h = (weight_in.shape[1], weight_mid.shape[1], weight_low.shape[1])
    wide = up(h[0], LANES)
    bias_wide = up(h[1], LANES) + up(h[2], LANES) + up(nf, LANES)
    w_shapes = [(wide, 32), (h[1], h[0] + 16), (h[2], h[1] + 16), (nf, h[2] + 16)]

    flowed, sent, counts, where, rest, w1, w2, w3, w4 = pl.pallas_call(
        functools.partial(flow_kernel, nf, cx, cy),
        out_shape=(jax.ShapeDtypeStruct((nf, cells, cz), f32),
                   jax.ShapeDtypeStruct(traffic, bf16),
                   jax.ShapeDtypeStruct((size, 1, LANES), jnp.int32),
                   jax.ShapeDtypeStruct((up(cells + 1, SUB * LANES) // LANES, LANES), jnp.int32),
                   jax.ShapeDtypeStruct((nf, LANES), f32))
        + tuple(jax.ShapeDtypeStruct(w, bf16) for w in w_shapes),
        in_specs=spec(pltpu.HBM, 11),
        out_specs=tuple(spec(pl.ANY) + spec(pltpu.VMEM, 8)),
        scratch_shapes=[pltpu.SMEM((1, listed), jnp.int32)]
        + [pltpu.VMEM((nf,) + box, f32)] * 3 + [
            pltpu.VMEM((3,) + box, f32),
            pltpu.VMEM((nf, room, cz), f32),
            pltpu.VMEM((6, cx, cy // SUB, SUB, cz), f32),
            pltpu.VMEM(traffic, bf16),
            pltpu.VMEM((1, LANES), jnp.int32),
            pltpu.VMEM((nf, h[0]), bf16),
            pltpu.VMEM((h[1], h[0]), bf16),
            pltpu.VMEM((h[2], h[1]), bf16),
            pltpu.VMEM((nf, h[2]), bf16),
            pltpu.VMEM((h[0],), f32),
            pltpu.VMEM((h[1],), f32),
            pltpu.VMEM((h[2],), f32),
            pltpu.VMEM((nf,), f32),
            pltpu.VMEM((32, wide), f32),
            pltpu.VMEM((32, bias_wide), f32),
            pltpu.VMEM((bias_wide, 32), bf16),
            pltpu.VMEM((h[0] + 16, LANES), bf16),
            pltpu.VMEM((h[1] + 16, LANES), bf16),
            pltpu.VMEM((h[2] + 16, LANES), bf16),
            pltpu.VMEM((2, cy, cz), f32),
            pltpu.VMEM((2, cx, cz), f32),
            pltpu.VMEM((2, cx, SUB, cz), f32),
            pltpu.VMEM((2, cx, cz), f32),
            pltpu.VMEM((cx, SUB, cz), f32),
        ] + halo_scratch(slots, cx, cy) + [
            dma((6,)), dma((6,)), dma((chunks, 4)), dma((chunks,)),
            dma((chunks + 1, size)), dma((chunks + 1, size)), dma((9,)),
            pltpu.SMEM((size, 1, LANES), jnp.int32), dma],
        compiler_params=pltpu.CompilerParams(
            collective_id=0, has_side_effects=True, vmem_limit_bytes=48 * MIB),
        name="flow",
    )(*[pltpu.with_memory_space_constraint(a, pltpu.HBM) for a in (
        react_list, fields, velocity, weight_in, weight_mid.T, weight_low.T, weight_out.T,
        bias_in, bias_mid, bias_low, bias_out)])

    group = 8
    n_lanes = group * LANES
    halves = size * cap // 2
    ret = pl.pallas_call(
        functools.partial(chem_kernel, nf, group, size),
        out_shape=jax.ShapeDtypeStruct((chunks, halves, 2 * SUB, LANES), bf16),
        in_specs=spec(pltpu.SMEM) + spec(pltpu.VMEM, 6),
        out_specs=spec(pltpu.VMEM)[0],
        scratch_shapes=[
            pltpu.SMEM((size * cap + 2 * group,), jnp.int32),
            pltpu.VMEM((nf + SUB, n_lanes), f32),
            pltpu.VMEM((h[0] + 16, n_lanes), bf16),
            pltpu.VMEM((h[1] + 16, n_lanes), bf16),
            pltpu.VMEM((h[2] + 16, n_lanes), bf16),
            pltpu.VMEM((nf, n_lanes), f32),
            pltpu.VMEM((chunks, size * cap + 1, SUB, LANES), f32),
        ],
        compiler_params=pltpu.CompilerParams(vmem_limit_bytes=40 * MIB),
        name="chem",
    )(counts, sent.reshape(chunks, halves, 2 * SUB, LANES), rest,
      w1, w2, w3, w4)

    most = max(lax.axis_size(a) for a in AXES) - 1
    updated, mine = pl.pallas_call(
        functools.partial(diffuse_kernel, nf, cx, cy),
        out_shape=(jax.ShapeDtypeStruct(fields.shape, f32),
                   jax.ShapeDtypeStruct((1,), f32)),
        in_specs=spec(pltpu.SMEM, 3) + spec(pl.ANY) + spec(pltpu.VMEM, 2),
        out_specs=(spec(pl.ANY)[0], spec(pltpu.SMEM)[0]),
        scratch_shapes=[
            pltpu.VMEM((nf,) + box, f32),
            pltpu.VMEM((nf, room, cz), f32),
            pltpu.VMEM((nf, cx, cy, cz), f32),
            pltpu.VMEM(traffic, bf16),
            pltpu.VMEM((chunks, size * cap + 1, SUB, LANES), f32),
            pltpu.VMEM((len(AXES), SUB, LANES), f32),
            pltpu.VMEM((len(AXES), most, SUB, LANES), f32),
            dma((len(AXES), most)),
            dma((len(AXES), most)),
        ] + halo_scratch(chunks, cx, cy) + [
            dma((chunks, size)), dma((chunks, size)), dma((chunks,)), dma((chunks,))],
        compiler_params=pltpu.CompilerParams(
            collective_id=1, has_side_effects=True, vmem_limit_bytes=48 * MIB),
        name="diffuse",
    )(diffusivity, where, owner_table[0], flowed, ret.reshape(traffic), rest)
    return updated, mine


def solution(mesh):
    return jax.shard_map(
        local,
        mesh=mesh,
        in_specs=(P(None, *AXES), P(None, *AXES)) + (P(),) * 9
        + (P(AXES, None), P(AXES, None)),
        out_specs=(P(None, *AXES), P(AXES)),
        check_vma=False,
    )
```
